128 devices in a mesh: dev: 128 (over y, x, z, core).
Axes of the slice: x: 4, y: 4, z: 4, core: 2. Of those that a mesh axis runs over, the one named last changes fastest.
Arguments:
- params: float32 [59, 262144], P(None, 'dev'), as said below
- blocks: int32 [512, 32], P('dev'), may hold values from 0 to 2047, as said below
- counts: int32 [512], P('dev'), may hold values from 4 to 32, as said below
- pixel_grad: float32 [3, 524288], P(None, 'dev'), may hold values from -192 to 192
Outputs:
- param_grad: float32 [59, 262144], P(None, 'dev')
The draws below stay inside these ranges and needn't reach their ends.
Inputs may be any that keep to these rules, and one draw needn't show every extreme that they name: Block b is owned by device b // 16. Within the tiles of one device no block appears twice, and for every owner exactly 1 of that device's 4 * 32 slots, used or not, name its blocks. `counts`: in every draw all tiles of some one device have 32 used slots. `params`: row 2, the depth, lies from 3 to 6; row 6 from 1 to 2; row 10 below -2.
All inputs are finite; a program needn't handle non-finite values.
Results may differ from the reference program's by a relative error of at most 0.0003.
Values sent between devices are 32-bit elements; how exact they have to be, the bound alone decides.
A program may use at most 128 MiB of HBM per device.

```python
import math
import jax
import jax.numpy as jnp
from jax import lax

BLOCK = 128
MAXB = 32
TILE_SIDE = 32
TILES_X = 32
TILE_DEV = 4
BLK_DEV = 16
TILE_PIX = 1024
TILES = 512
PIX = 524288
GAUSS = 262144
IMG_W = 1024
IMG_H = 512


def block_table(key):
    devices = TILES // TILE_DEV
    slots = TILE_DEV * MAXB
    device_keys = jax.random.split(jax.random.fold_in(key, 11), devices)
    perms = jax.vmap(lambda single: jax.random.permutation(single, devices))(device_keys)
    offsets = jax.random.randint(jax.random.fold_in(key, 12), (devices, devices), 0, BLK_DEV)
    positions = jnp.arange(slots, dtype=jnp.int32)
    owners = perms[:, positions % devices]
    starts = jnp.take_along_axis(offsets, owners, axis=1)
    local_ids = (starts + positions[None, :] // devices) % BLK_DEV
    return (owners * BLK_DEV + local_ids).reshape(TILES, MAXB).astype(jnp.int32)


def draw_blocks(key, part):
    return block_table(key)


def draw_counts(key, part):
    devices = TILES // TILE_DEV
    heavy_dev = jax.random.randint(jax.random.fold_in(key, 21), (), 0, devices)
    light_counts = jax.random.randint(jax.random.fold_in(key, 22), (TILES,), MAXB // 8, 2 * MAXB // 3 + 1)
    device_of = jnp.arange(TILES, dtype=jnp.int32) // TILE_DEV
    return jnp.where(device_of == heavy_dev, MAXB, light_counts).astype(jnp.int32)


def draw_params(key, part):
    subkeys = jax.random.split(jax.random.fold_in(key, 31), 8)
    depths = jax.random.uniform(subkeys[0], (GAUSS,), jnp.float32, 3.0, 6.0)
    screen_u = jax.random.uniform(subkeys[1], (GAUSS,), jnp.float32, 0.0, 1.0 * IMG_W)
    screen_v = jax.random.uniform(subkeys[2], (GAUSS,), jnp.float32, 0.0, 1.0 * IMG_H)
    mean_x = (screen_u - IMG_W / 2.0) * depths / IMG_W
    mean_y = (screen_v - IMG_H / 2.0) * depths / IMG_W
    log_scales = jax.random.uniform(subkeys[3], (3, GAUSS), jnp.float32, -1.6, -0.6)
    quat_r = jax.random.uniform(subkeys[4], (1, GAUSS), jnp.float32, 1.0, 2.0)
    quat_rest = jax.random.uniform(subkeys[5], (3, GAUSS), jnp.float32, -1.5, 1.5)
    total_slots = MAXB * BLOCK
    opacity_raw = jax.random.uniform(subkeys[6], (1, GAUSS), jnp.float32, math.log(2.0 / total_slots), math.log(32.0 / total_slots))
    harmonics = 0.25 * jax.random.normal(subkeys[7], (48, GAUSS), jnp.float32)
    dc_scale = jnp.where(jnp.arange(48) % 16 == 0, 2.0, 1.0).astype(jnp.float32)[:, None]
    harmonics = harmonics * dc_scale
    return jnp.concatenate([mean_x[None], mean_y[None], depths[None], log_scales, quat_r, quat_rest, opacity_raw, harmonics], axis=0).astype(jnp.float32)


def shard_levels(own_key, dims, shards, low, largest):
    def one(dim, shards_of):
        draws = jax.random.uniform(jax.random.fold_in(jax.random.fold_in(own_key, 6), dim), (shards_of,), jnp.float32, low / len(shards), largest / len(shards))
        return jnp.repeat(jnp.exp(draws), dims[dim] // shards_of).reshape((-1,) + (1,) * (len(dims) - dim - 1))

    loudness = one(*shards[0])
    for cut in shards[1:]:
        loudness = loudness * one(*cut)
    return loudness


def normal_values(own_key, shape, width, limit, shards=(), kind=jnp.bfloat16):
    array = jax.random.normal(own_key, shape, jnp.float32) * width
    if len(shards) > 0:
        array = shard_levels(own_key, shape, shards, -0.22, 0.18) * array
    return jnp.clip(array, min=-limit, max=limit).astype(kind)


def setup_inputs(seed: int = 0) -> dict:
    keys = jax.random.split(jax.random.key(seed), 5)
    params = draw_params(jax.random.fold_in(keys[4], 71), 0)
    blocks = draw_blocks(jax.random.fold_in(keys[4], 71), 0)
    counts = draw_counts(jax.random.fold_in(keys[4], 71), 0)
    pixel_grad = normal_values(keys[3], (3, PIX), 32.0, 192.0, ((1, 128),), jnp.float32)
    return {"params": params, "blocks": blocks, "counts": counts, "pixel_grad": pixel_grad}


sh_zero = 0.28209479177387814
sh_one = 0.4886025119029199
sh_two = [1.0925484305920792, -1.0925484305920792, 0.31539156525252005, -1.0925484305920792, 0.5462742152960396]
sh_three = [-0.5900435899266435, 2.890611442640554, -0.4570457994644658, 0.3731763325901154, -0.4570457994644658, 1.445305721320277, -0.5900435899266435]

def sh_basis(dir_x, dir_y, dir_z):
    sq_x = dir_x * dir_x
    sq_y = dir_y * dir_y
    sq_z = dir_z * dir_z
    return [sh_zero + 0.0 * dir_x, -sh_one * dir_y, sh_one * dir_z, -sh_one * dir_x, sh_two[0] * dir_x * dir_y, sh_two[1] * dir_y * dir_z, sh_two[2] * (2.0 * sq_z - sq_x - sq_y), sh_two[3] * dir_x * dir_z, sh_two[4] * (sq_x - sq_y), sh_three[0] * dir_y * (3.0 * sq_x - sq_y), sh_three[1] * dir_x * dir_y * dir_z, sh_three[2] * dir_y * (4.0 * sq_z - sq_x - sq_y), sh_three[3] * dir_z * (2.0 * sq_z - 3.0 * sq_x - 3.0 * sq_y), sh_three[4] * dir_x * (4.0 * sq_z - sq_x - sq_y), sh_three[5] * dir_z * (sq_x - sq_y), sh_three[6] * dir_x * (sq_x - 3.0 * sq_y)]

def screen(params, focal_len, centre_x, centre_y):
    mean_x, mean_y, depths = (params[0], params[1], params[2])
    scales = jnp.exp(params[3:6])
    quat = params[6:10]
    quat = quat / jnp.sqrt(lax.optimization_barrier(jnp.sum(quat * quat, axis=0)))
    quat_r, quat_i, quat_j, quat_k = (quat[0], quat[1], quat[2], quat[3])
    rotation = [[1.0 - 2.0 * (quat_j * quat_j + quat_k * quat_k), 2.0 * (quat_i * quat_j - quat_r * quat_k), 2.0 * (quat_i * quat_k + quat_r * quat_j)], [2.0 * (quat_i * quat_j + quat_r * quat_k), 1.0 - 2.0 * (quat_i * quat_i + quat_k * quat_k), 2.0 * (quat_j * quat_k - quat_r * quat_i)], [2.0 * (quat_i * quat_k - quat_r * quat_j), 2.0 * (quat_j * quat_k + quat_r * quat_i), 1.0 - 2.0 * (quat_i * quat_i + quat_j * quat_j)]]
    inv_z = 1.0 / depths
    diag_jac = focal_len * inv_z
    side_x = -focal_len * mean_x * inv_z * inv_z
    side_y = -focal_len * mean_y * inv_z * inv_z
    upper = [(diag_jac * rotation[0][column] + side_x * rotation[2][column]) * scales[column] for column in range(3)]
    lower = [(diag_jac * rotation[1][column] + side_y * rotation[2][column]) * scales[column] for column in range(3)]
    cov_xx = upper[0] * upper[0] + upper[1] * upper[1] + upper[2] * upper[2] + 0.3
    cov_xy = upper[0] * lower[0] + upper[1] * lower[1] + upper[2] * lower[2]
    cov_yy = lower[0] * lower[0] + lower[1] * lower[1] + lower[2] * lower[2] + 0.3
    determ = cov_xx * cov_yy - cov_xy * cov_xy
    screen_u = focal_len * mean_x * inv_z + centre_x
    screen_v = focal_len * mean_y * inv_z + centre_y
    opacity = jax.nn.sigmoid(params[10])
    distance = jnp.sqrt(mean_x * mean_x + mean_y * mean_y + depths * depths)
    basis = sh_basis(mean_x / distance, mean_y / distance, depths / distance)
    colors = [0.5 + sum((basis[harmonic] * params[11 + 16 * channel + harmonic] for harmonic in range(16))) for channel in range(3)]
    features = jnp.stack([screen_u, screen_v, cov_yy / determ, -cov_xy / determ, cov_xx / determ, opacity] + colors, axis=0)
    return features.reshape(9, -1, BLOCK).transpose(1, 0, 2)

def pixel_coords(tile_id):
    positions = jnp.arange(TILE_SIDE * TILE_SIDE, dtype=jnp.int32)
    pix_x = (tile_id % TILES_X * TILE_SIDE + positions % TILE_SIDE).astype(jnp.float32) + 0.5
    pix_y = (tile_id // TILES_X * TILE_SIDE + positions // TILE_SIDE).astype(jnp.float32) + 0.5
    return (pix_x, pix_y)

def pair_terms(feature, pix_x, pix_y):
    off_x = pix_x[:, None] - feature[0][None, :]
    off_y = pix_y[:, None] - feature[1][None, :]
    exponent = -0.5 * (feature[2][None, :] * off_x * off_x + feature[4][None, :] * off_y * off_y) - feature[3][None, :] * off_x * off_y
    falloff = jnp.exp(exponent)
    return (off_x, off_y, falloff, feature[5][None, :] * falloff)

def tile_gradients(listed, live_count, cotangent, pix_x, pix_y):
    precise = lax.Precision.HIGHEST
    pixels = pix_x.shape[0]

    def forward(slot_idx, state_in):
        log_trans, colors = state_in
        feature = listed[slot_idx]
        alphas = pair_terms(feature, pix_x, pix_y)[3]
        log_keep = jnp.log(1.0 - alphas)
        before = jnp.cumsum(log_keep, axis=1) - log_keep
        weight = jnp.exp(log_trans[:, None] + before) * alphas
        colors = colors + jnp.dot(weight, feature[6:9].T, precision=precise)
        return (log_trans + lax.optimization_barrier(jnp.sum(log_keep, axis=1)), colors)
    start_state = (jnp.zeros((pixels,), jnp.float32), jnp.zeros((pixels, 3), jnp.float32))
    image = lax.fori_loop(0, live_count, forward, start_state)[1]

    def backward(slot_idx, state_in):
        log_trans, done, gradients = state_in
        feature = listed[slot_idx]
        off_x, off_y, falloff, alphas = pair_terms(feature, pix_x, pix_y)
        log_keep = jnp.log(1.0 - alphas)
        before = jnp.cumsum(log_keep, axis=1) - log_keep
        transmit = jnp.exp(log_trans[:, None] + before)
        weight = transmit * alphas
        dalpha = jnp.zeros_like(alphas)
        for channel in range(3):
            shaded = weight * feature[6 + channel][None, :]
            behind = (image[:, channel] - done[:, channel])[:, None] - jnp.cumsum(shaded, axis=1)
            dalpha = dalpha + cotangent[channel][:, None] * (transmit * feature[6 + channel][None, :] - behind / (1.0 - alphas))
        dcolor = jnp.dot(cotangent, weight, precision=precise)
        dpower = dalpha * alphas
        sums_list = [lax.optimization_barrier(jnp.sum(dpower * (feature[2][None, :] * off_x + feature[3][None, :] * off_y), axis=0)), lax.optimization_barrier(jnp.sum(dpower * (feature[3][None, :] * off_x + feature[4][None, :] * off_y), axis=0)), -0.5 * lax.optimization_barrier(jnp.sum(dpower * off_x * off_x, axis=0)), -lax.optimization_barrier(jnp.sum(dpower * off_x * off_y, axis=0)), -0.5 * lax.optimization_barrier(jnp.sum(dpower * off_y * off_y, axis=0)), lax.optimization_barrier(jnp.sum(dalpha * falloff, axis=0))]
        block_grad = jnp.concatenate([jnp.stack(sums_list, axis=0), dcolor], axis=0)
        gradients = lax.dynamic_update_index_in_dim(gradients, block_grad, slot_idx, 0)
        done = done + jnp.dot(weight, feature[6:9].T, precision=precise)
        return (log_trans + lax.optimization_barrier(jnp.sum(log_keep, axis=1)), done, gradients)
    return lax.fori_loop(0, live_count, backward, (start_state[0], start_state[1], jnp.zeros_like(listed)))[2]

def reference(params, blocks, counts, pixel_grad):
    features, pullback = jax.vjp(lambda values: screen(values, float(IMG_W), IMG_W / 2.0, IMG_H / 2.0), params)
    cotangent = pixel_grad.reshape(3, TILES, TILE_PIX).transpose(1, 0, 2)

    def one_tile(tile_args):
        tile_id, row_ids, live_count, tile_cot = tile_args
        pix_x, pix_y = pixel_coords(tile_id)
        return tile_gradients(features[row_ids], live_count, tile_cot, pix_x, pix_y)
    gradients = lax.map(one_tile, (jnp.arange(TILES, dtype=jnp.int32), blocks, counts, cotangent))
    feature_grad = jnp.zeros_like(features).at[blocks.reshape(-1)].add(gradients.reshape(-1, 9, BLOCK))
    return pullback(feature_grad)[0]
```

```python
import jax
import jax.numpy as jnp
from jax import lax
from jax.experimental import pallas as pl
from jax.experimental.pallas import tpu as pltpu
from jax.sharding import PartitionSpec as P

LOG2E = 1.4426950408889634
sh_zero = 0.28209479177387814
sh_one = 0.4886025119029199
sh_two = [
    1.0925484305920792,
    -1.0925484305920792,
    0.31539156525252005,
    -1.0925484305920792,
    0.5462742152960396,
]
sh_three = [
    -0.5900435899266435,
    2.890611442640554,
    -0.4570457994644658,
    0.3731763325901154,
    -0.4570457994644658,
    1.445305721320277,
    -0.5900435899266435,
]


def sh_basis(dir_x, dir_y, dir_z):
    sq_x = dir_x * dir_x
    sq_y = dir_y * dir_y
    sq_z = dir_z * dir_z
    return [
        sh_zero + 0.0 * dir_x,
        -sh_one * dir_y,
        sh_one * dir_z,
        -sh_one * dir_x,
        sh_two[0] * dir_x * dir_y,
        sh_two[1] * dir_y * dir_z,
        sh_two[2] * (2.0 * sq_z - sq_x - sq_y),
        sh_two[3] * dir_x * dir_z,
        sh_two[4] * (sq_x - sq_y),
        sh_three[0] * dir_y * (3.0 * sq_x - sq_y),
        sh_three[1] * dir_x * dir_y * dir_z,
        sh_three[2] * dir_y * (4.0 * sq_z - sq_x - sq_y),
        sh_three[3] * dir_z * (2.0 * sq_z - 3.0 * sq_x - 3.0 * sq_y),
        sh_three[4] * dir_x * (4.0 * sq_z - sq_x - sq_y),
        sh_three[5] * dir_z * (sq_x - sq_y),
        sh_three[6] * dir_x * (sq_x - 3.0 * sq_y),
    ]


def screen(params, focal_len, centre_x, centre_y):
    mean_x, mean_y, depths = (params[0], params[1], params[2])
    scales = [jnp.exp(params[row]) for row in range(3, 6)]
    quat = params[6:10]
    norm = jnp.sqrt(quat[0] * quat[0] + quat[1] * quat[1] + quat[2] * quat[2] + quat[3] * quat[3])
    quat = [part / norm for part in quat]
    quat_r, quat_i, quat_j, quat_k = (quat[0], quat[1], quat[2], quat[3])
    rotation = [
        [
            1.0 - 2.0 * (quat_j * quat_j + quat_k * quat_k),
            2.0 * (quat_i * quat_j - quat_r * quat_k),
            2.0 * (quat_i * quat_k + quat_r * quat_j),
        ],
        [
            2.0 * (quat_i * quat_j + quat_r * quat_k),
            1.0 - 2.0 * (quat_i * quat_i + quat_k * quat_k),
            2.0 * (quat_j * quat_k - quat_r * quat_i),
        ],
        [
            2.0 * (quat_i * quat_k - quat_r * quat_j),
            2.0 * (quat_j * quat_k + quat_r * quat_i),
            1.0 - 2.0 * (quat_i * quat_i + quat_j * quat_j),
        ],
    ]
    inv_z = 1.0 / depths
    diag_jac = focal_len * inv_z
    side_x = -focal_len * mean_x * inv_z * inv_z
    side_y = -focal_len * mean_y * inv_z * inv_z
    upper = [
        (diag_jac * rotation[0][column] + side_x * rotation[2][column]) * scales[column]
        for column in range(3)
    ]
    lower = [
        (diag_jac * rotation[1][column] + side_y * rotation[2][column]) * scales[column]
        for column in range(3)
    ]
    cov_xx = upper[0] * upper[0] + upper[1] * upper[1] + upper[2] * upper[2] + 0.3
    cov_xy = upper[0] * lower[0] + upper[1] * lower[1] + upper[2] * lower[2]
    cov_yy = lower[0] * lower[0] + lower[1] * lower[1] + lower[2] * lower[2] + 0.3
    determ = cov_xx * cov_yy - cov_xy * cov_xy
    screen_u = focal_len * mean_x * inv_z + centre_x
    screen_v = focal_len * mean_y * inv_z + centre_y
    logit = params[10]
    log_opacity = (logit - jnp.log1p(jnp.exp(logit))) * LOG2E
    distance = jnp.sqrt(mean_x * mean_x + mean_y * mean_y + depths * depths)
    basis = sh_basis(mean_x / distance, mean_y / distance, depths / distance)
    colors = [
        0.5
        + sum((basis[harmonic] * params[11 + 16 * channel + harmonic] for harmonic in range(16)))
        for channel in range(3)
    ]
    return [screen_u, screen_v, cov_yy / determ, -cov_xy / determ, cov_xx / determ, log_opacity] + colors
BLOCK=128; SIDE=32; TX=32; PIX=1024; MAXB=32
f32=jnp.float32; bf16=jnp.bfloat16

def split3(x):
    hi=x.astype(bf16).astype(f32); r=x-hi
    mid=r.astype(bf16).astype(f32); lo=r-mid
    return hi,mid,lo

def tiles_kernel(blocks_ref, counts_ref, feat_ref, cot_ref, out_ref,
                 fs, xs, lhs, rhs, red, eq, al, ws, qs, eb, res):
    first_tile=lax.axis_index("dev")*4
    lane=lax.broadcasted_iota(jnp.int32,(1,PIX),1)
    X=(lane%SIDE-16).astype(f32); Y=(lane//SIDE-16).astype(f32)
    mono=[X*X,X*Y,Y*Y,X,Y,jnp.ones_like(X)]
    out_ref[...]=jnp.zeros_like(out_ref)
    rhs[...]=jnp.zeros_like(rhs)
    for part in range(3):
        for k in range(6): rhs[16*part+k:16*part+k+1,0:PIX]=mono[k]
    eb_zero=None
    def tile(ti,_):
        cnt=counts_ref[ti]
        tid=first_tile+ti
        cx=((tid%TX)*SIDE).astype(f32)+16.5
        cy=((tid//TX)*SIDE).astype(f32)+16.5
        def gat(t,_):
            ow=blocks_ref[ti,t]//16
            for f in range(9): fs[f,pl.ds(t,1),:]=feat_ref[ow,f]
            return 0
        lax.fori_loop(0,cnt,gat,0)
        u=fs[0]-cx; v=fs[1]-cy; A=fs[2]; B=fs[3]; C=fs[4]; lo2=fs[5]
        p=A*u+B*v; r=B*u+C*v
        cf=[(-0.5*LOG2E)*A,(-LOG2E)*B,(-0.5*LOG2E)*C,LOG2E*p,LOG2E*r,(-0.5*LOG2E)*(u*p+v*r)+lo2,
            fs[6],fs[7],fs[8],fs[6],fs[7],fs[8],fs[6],fs[7],fs[8]]
        for k in range(15): xs[:,k,:]=cf[k]
        xs[:,15,:]=jnp.zeros_like(u)
        for c in range(3):
            ct=cot_ref[c:c+1,pl.ds(pl.multiple_of(ti*PIX,PIX),PIX)]
            h,m,l=split3(ct)
            for part in range(3):
                b=16*part+6+c
                rhs[b:b+1,PIX:]=h; rhs[b+3:b+4,PIX:]=m; rhs[b+6:b+7,PIX:]=l
        R=jnp.concatenate([rhs[0:6,0:PIX],rhs[6:15,PIX:],jnp.zeros((1,PIX),f32)],axis=0)
        red[...]=jnp.concatenate([R,jnp.zeros((112,PIX),f32)],axis=0).T.astype(bf16)
        def slotp(t,_):
            x=xs[t]
            h,m,l=split3(x)
            y=jnp.concatenate([h,m,l,jnp.zeros((80,128),f32)],axis=0).T
            for k in range(8):
                mm=t*8+k
                s=mm//cnt; j0=16*(mm%cnt)
                lhs[pl.ds(j0*8+s,16,stride=8),:]=y[16*k:16*k+16,:]
            return 0
        lax.fori_loop(0,cnt,slotp,0)
        rb=rhs[...].astype(bf16)
        def fwd(b,st):
            T,Cc=st
            L=lhs[pl.ds(pl.multiple_of(b*128,128),128),0:48].astype(bf16)
            eq[...]=jnp.dot(L,rb,preferred_element_type=f32)
            for jj in range(16):
                rs=pl.ds(pl.multiple_of(b*128+8*jj,8),8)
                a=jnp.exp2(eq[8*jj:8*jj+8,0:PIX])
                q=eq[8*jj:8*jj+8,PIX:]
                w=T*a; T=T-w; Cc=Cc+w*q
                al[rs,:]=a; ws[rs,:]=w; qs[rs,:]=q
            return T,Cc
        K,Cc=lax.fori_loop(0,cnt,fwd,(jnp.ones((8,PIX),f32),jnp.zeros((8,PIX),f32)))
        P=[jnp.ones((1,PIX),f32)]
        for s in range(7): P.append(P[-1]*K[s:s+1])
        V=[jnp.zeros((1,PIX),f32)]
        for s in range(7,0,-1): V.append(Cc[s:s+1]+K[s:s+1]*V[-1])
        Pv=jnp.concatenate(P,axis=0); V0=jnp.concatenate(V[::-1],axis=0)
        lane128=lax.broadcasted_iota(jnp.int32,(128,128),1)
        def bwd(i,V):
            b=cnt-1-i
            for jp in range(7,-1,-1):
                es=[None,None]; wv=[None,None]
                for h in (1,0):
                    rs=pl.ds(pl.multiple_of(b*128+16*jp+8*h,8),8)
                    d=qs[rs,:]-V
                    w=ws[rs,:]*Pv
                    es[h]=w*d; wv[h]=w
                    V=V+al[rs,:]*d
                e2=jnp.concatenate(es,axis=0); w2=jnp.concatenate(wv,axis=0)
                eh=e2.astype(bf16); wh=w2.astype(bf16)
                eb[16*jp:16*jp+16,:]=eh
                eb[128+16*jp:128+16*jp+16,:]=(e2-eh.astype(f32)).astype(bf16)
                eb[256+16*jp:256+16*jp+16,:]=wh
                eb[384+16*jp:384+16*jp+16,:]=(w2-wh.astype(f32)).astype(bf16)
            rr=jnp.dot(eb[...],red[...],preferred_element_type=f32)
            o=jnp.where(lane128<6,rr[0:128]+rr[128:256],rr[256:384]+rr[384:512])
            res[pl.ds(pl.multiple_of(b*128,128),128),:]=o
            return V
        lax.fori_loop(0,cnt,bwd,V0)
        def slote(t,_):
            ow=blocks_ref[ti,t]//16
            ps=[]
            for k in range(8):
                mm=t*8+k
                s=mm//cnt; j0=16*(mm%cnt)
                ps.append(res[pl.ds(j0*8+s,16,stride=8),:])
            M=jnp.concatenate(ps,axis=0).T[0:16,:]
            row=lambda k: M[k:k+1,:]
            mxx,mxy,myy,mx,my,m1=[row(k) for k in range(6)]
            ff=lambda f: feat_ref[ow,f]
            u=ff(0)-cx; v=ff(1)-cy; A=ff(2); B=ff(3); C=ff(4)
            sx=mx-u*m1; sy=my-v*m1
            sxx=mxx-2.0*u*mx+u*u*m1
            syy=myy-2.0*v*my+v*v*m1
            sxy=mxy-u*my-v*mx+u*v*m1
            o=[A*sx+B*sy,B*sx+C*sy,-0.5*sxx,-sxy,-0.5*syy,m1]+[row(6+c)+row(9+c)+row(12+c) for c in range(3)]
            for f in range(9): out_ref[ow,f]=o[f]
            return 0
        lax.fori_loop(0,cnt,slote,0)
        return 0
    lax.fori_loop(0,4,tile,0)
def tiles(blocks,counts,feat,cot):
    sm=pl.BlockSpec(memory_space=pltpu.SMEM); vm=pl.BlockSpec(memory_space=pltpu.VMEM)
    return pl.pallas_call(tiles_kernel,out_shape=jax.ShapeDtypeStruct((128,9,1,128),f32),
        in_specs=[sm,sm,vm,vm],out_specs=vm,
        scratch_shapes=[pltpu.VMEM((9,32,128),f32),pltpu.VMEM((32,16,128),f32),pltpu.VMEM((4096,128),f32),
            pltpu.VMEM((48,2*PIX),f32),pltpu.VMEM((PIX,128),bf16),pltpu.VMEM((128,2*PIX),f32),
            pltpu.VMEM((4096,PIX),f32),pltpu.VMEM((4096,PIX),f32),pltpu.VMEM((4096,PIX),f32),
            pltpu.VMEM((512,PIX),bf16),pltpu.VMEM((4096,128),f32)],
        compiler_params=pltpu.CompilerParams(vmem_limit_bytes=67043328))(blocks,counts,feat,cot)


def load_params(p_ref):
    return [p_ref[row : row + 1, :].reshape(16, BLOCK) for row in range(59)]


def screen_rows(rows):
    return screen(rows, 1024.0, 512.0, 256.0)


def prep_kernel(idx_ref, p_ref, send_ref, fsc):
    for f, value in enumerate(screen_rows(load_params(p_ref))):
        fsc[f] = jnp.maximum(value, -1000.0) if f == 5 else value

    def put(d, _):
        for f in range(9):
            send_ref[d, f] = fsc[f, pl.ds(idx_ref[d], 1), :]
        return 0

    lax.fori_loop(0, 128, put, 0)


def final_kernel(idx_ref, p_ref, recv_ref, out_ref, acc):
    acc[...] = jnp.zeros_like(acc)

    def add(d, _):
        for f in range(9):
            acc[f, pl.ds(idx_ref[d], 1), :] = acc[f, pl.ds(idx_ref[d], 1), :] + recv_ref[d, f]
        return 0

    lax.fori_loop(0, 128, add, 0)
    pullback = jax.vjp(screen_rows, load_params(p_ref))[1]
    grads = [acc[f] for f in range(9)]
    grads[5] = grads[5] * (1.0 / LOG2E)
    for row, value in enumerate(pullback(grads)[0]):
        out_ref[row : row + 1, :] = value.reshape(1, 2048)


def exchange_kernel(x_ref, o_ref, ssem, rsem, lsem):
    n = lax.axis_size("dev")
    me = lax.axis_index("dev")
    bar = pltpu.get_barrier_semaphore()

    def sig(k, _):
        pl.semaphore_signal(bar, inc=1, device_id=(lax.rem(me + k, n),), device_id_type=pl.DeviceIdType.MESH)
        return 0

    lax.fori_loop(1, n, sig, 0)
    own = pltpu.make_async_copy(x_ref.at[me], o_ref.at[me], lsem)
    own.start()
    pl.semaphore_wait(bar, n - 1)

    def snd(k, _):
        peer = lax.rem(me + k, n)
        pltpu.make_async_remote_copy(
            src_ref=x_ref.at[peer],
            dst_ref=o_ref.at[me],
            send_sem=ssem,
            recv_sem=rsem,
            device_id=(peer,),
            device_id_type=pl.DeviceIdType.MESH,
        ).start()
        return 0

    lax.fori_loop(1, n, snd, 0)
    own.wait()
    most = pl.ds(0, n - 1)
    pltpu.make_async_copy(x_ref.at[most], x_ref.at[most], ssem).wait()
    pltpu.make_async_copy(o_ref.at[most], o_ref.at[most], rsem).wait()


def exchange(x, cid):
    vm = pl.BlockSpec(memory_space=pltpu.VMEM)
    return pl.pallas_call(
        exchange_kernel,
        out_shape=jax.ShapeDtypeStruct(x.shape, x.dtype),
        in_specs=[vm],
        out_specs=vm,
        scratch_shapes=[pltpu.SemaphoreType.DMA] * 3,
        compiler_params=pltpu.CompilerParams(collective_id=cid, has_side_effects=True),
    )(x)


def body(params, blocks, counts, pixel_grad):
    sm = pl.BlockSpec(memory_space=pltpu.SMEM)
    vm = pl.BlockSpec(memory_space=pltpu.VMEM)
    flat = blocks.reshape(-1)
    named = flat[:, None] // 16 == jnp.arange(128, dtype=jnp.int32)[None, :]
    want = jnp.sum(jnp.where(named, flat[:, None] % 16, 0), axis=0)
    asked = lax.all_to_all(want, "dev", 0, 0, tiled=True)
    send = pl.pallas_call(
        prep_kernel,
        out_shape=jax.ShapeDtypeStruct((128, 9, 1, 128), f32),
        in_specs=[sm, vm],
        out_specs=vm,
        scratch_shapes=[pltpu.VMEM((9, 16, 128), f32)],
    )(asked, params)
    feat = exchange(send, 0)
    grads = tiles(blocks, counts, feat, pixel_grad)
    back = exchange(grads, 1)
    return pl.pallas_call(
        final_kernel,
        out_shape=jax.ShapeDtypeStruct((59, 2048), f32),
        in_specs=[sm, vm, vm],
        out_specs=vm,
        scratch_shapes=[pltpu.VMEM((9, 16, 128), f32)],
    )(asked, params, back)


def solution(mesh):
    return jax.shard_map(
        body,
        mesh=mesh,
        in_specs=(P(None, "dev"), P("dev", None), P("dev"), P(None, "dev")),
        out_specs=P(None, "dev"),
        check_vma=False,
    )
```

```python
import jax
import jax.numpy as jnp
from jax import lax
from jax.experimental import pallas as pl
from jax.experimental.pallas import tpu as pltpu
from jax.sharding import PartitionSpec as P

LOG2E = 1.4426950408889634
sh_zero = 0.28209479177387814
sh_one = 0.4886025119029199
sh_two = [
    1.0925484305920792,
    -1.0925484305920792,
    0.31539156525252005,
    -1.0925484305920792,
    0.5462742152960396,
]
sh_three = [
    -0.5900435899266435,
    2.890611442640554,
    -0.4570457994644658,
    0.3731763325901154,
    -0.4570457994644658,
    1.445305721320277,
    -0.5900435899266435,
]


def sh_basis(dir_x, dir_y, dir_z):
    sq_x = dir_x * dir_x
    sq_y = dir_y * dir_y
    sq_z = dir_z * dir_z
    return [
        sh_zero + 0.0 * dir_x,
        -sh_one * dir_y,
        sh_one * dir_z,
        -sh_one * dir_x,
        sh_two[0] * dir_x * dir_y,
        sh_two[1] * dir_y * dir_z,
        sh_two[2] * (2.0 * sq_z - sq_x - sq_y),
        sh_two[3] * dir_x * dir_z,
        sh_two[4] * (sq_x - sq_y),
        sh_three[0] * dir_y * (3.0 * sq_x - sq_y),
        sh_three[1] * dir_x * dir_y * dir_z,
        sh_three[2] * dir_y * (4.0 * sq_z - sq_x - sq_y),
        sh_three[3] * dir_z * (2.0 * sq_z - 3.0 * sq_x - 3.0 * sq_y),
        sh_three[4] * dir_x * (4.0 * sq_z - sq_x - sq_y),
        sh_three[5] * dir_z * (sq_x - sq_y),
        sh_three[6] * dir_x * (sq_x - 3.0 * sq_y),
    ]


def screen(params, focal_len, centre_x, centre_y):
    mean_x, mean_y, depths = (params[0], params[1], params[2])
    scales = [jnp.exp(params[row]) for row in range(3, 6)]
    quat = params[6:10]
    norm = jnp.sqrt(quat[0] * quat[0] + quat[1] * quat[1] + quat[2] * quat[2] + quat[3] * quat[3])
    quat = [part / norm for part in quat]
    quat_r, quat_i, quat_j, quat_k = (quat[0], quat[1], quat[2], quat[3])
    rotation = [
        [
            1.0 - 2.0 * (quat_j * quat_j + quat_k * quat_k),
            2.0 * (quat_i * quat_j - quat_r * quat_k),
            2.0 * (quat_i * quat_k + quat_r * quat_j),
        ],
        [
            2.0 * (quat_i * quat_j + quat_r * quat_k),
            1.0 - 2.0 * (quat_i * quat_i + quat_k * quat_k),
            2.0 * (quat_j * quat_k - quat_r * quat_i),
        ],
        [
            2.0 * (quat_i * quat_k - quat_r * quat_j),
            2.0 * (quat_j * quat_k + quat_r * quat_i),
            1.0 - 2.0 * (quat_i * quat_i + quat_j * quat_j),
        ],
    ]
    inv_z = 1.0 / depths
    diag_jac = focal_len * inv_z
    side_x = -focal_len * mean_x * inv_z * inv_z
    side_y = -focal_len * mean_y * inv_z * inv_z
    upper = [
        (diag_jac * rotation[0][column] + side_x * rotation[2][column]) * scales[column]
        for column in range(3)
    ]
    lower = [
        (diag_jac * rotation[1][column] + side_y * rotation[2][column]) * scales[column]
        for column in range(3)
    ]
    cov_xx = upper[0] * upper[0] + upper[1] * upper[1] + upper[2] * upper[2] + 0.3
    cov_xy = upper[0] * lower[0] + upper[1] * lower[1] + upper[2] * lower[2]
    cov_yy = lower[0] * lower[0] + lower[1] * lower[1] + lower[2] * lower[2] + 0.3
    determ = cov_xx * cov_yy - cov_xy * cov_xy
    screen_u = focal_len * mean_x * inv_z + centre_x
    screen_v = focal_len * mean_y * inv_z + centre_y
    logit = params[10]
    log_opacity = (logit - jnp.log1p(jnp.exp(logit))) * LOG2E
    distance = jnp.sqrt(mean_x * mean_x + mean_y * mean_y + depths * depths)
    basis = sh_basis(mean_x / distance, mean_y / distance, depths / distance)
    colors = [
        0.5
        + sum((basis[harmonic] * params[11 + 16 * channel + harmonic] for harmonic in range(16)))
        for channel in range(3)
    ]
    return [screen_u, screen_v, cov_yy / determ, -cov_xy / determ, cov_xx / determ, log_opacity] + colors
BLOCK=128; SIDE=32; TX=32; PIX=1024; MAXB=32
BU=4; FJ=4; BJ=4
f32=jnp.float32; bf16=jnp.bfloat16

def split3(x):
    hi=x.astype(bf16).astype(f32); r=x-hi
    mid=r.astype(bf16).astype(f32); lo=r-mid
    return hi,mid,lo

def tiles_kernel(blocks_ref, counts_ref, feat_ref, cot_ref, out_ref,
                 fs, xs, lhs, rhs, wa, wb, pref, vref, st, cots, rbs, al, ws, eA, eB, sbA, zbA, sbB, zbB, res):
    first_tile=lax.axis_index("dev")*4
    lane=lax.broadcasted_iota(jnp.int32,(1,PIX),1)
    X=(lane%SIDE-16).astype(f32); Y=(lane//SIDE-16).astype(f32)
    mono=[X*X,X*Y,Y*Y,X,Y,jnp.ones_like(X)]
    out_ref[...]=jnp.zeros_like(out_ref)
    rhs[...]=jnp.zeros_like(rhs)
    for part in range(3):
        for k in range(6): rhs[16*part+k:16*part+k+1,0:PIX]=mono[k]
    x1=X[:,0:128]; y1=(lax.broadcasted_iota(jnp.int32,(1,128),1)//SIDE-16).astype(f32); o1=jnp.ones_like(x1); z1=jnp.zeros_like(x1)
    pad=jnp.zeros((80,128),f32)
    rep=lambda rows: jnp.concatenate([jnp.broadcast_to(x,(8,128)) for x in rows]+[pad],axis=0).T
    W0=rep([x1*x1,x1*y1,y1*y1,x1,y1,o1])
    W1=rep([z1,4.0*x1,8.0*y1-16.0,z1,4.0*o1,z1])
    W2=rep([z1,z1,32.0*o1,z1,z1,z1])
    wa[...]=jnp.concatenate([W0,W1],axis=0).astype(bf16)
    wb[...]=jnp.concatenate([W2,W2],axis=0).astype(bf16)
    def tile(ti,_):
        cnt=counts_ref[ti]
        tid=first_tile+ti
        cx=((tid%TX)*SIDE).astype(f32)+16.5
        cy=((tid//TX)*SIDE).astype(f32)+16.5
        last=128*cnt
        def step_row(r):
            r=r+128
            return jnp.where(r>=last,r-last+1,r)
        def gat(t,_):
            ow=blocks_ref[ti,t]//16
            for f in range(9): fs[f,pl.ds(t,1),:]=feat_ref[ow,f]
            return 0
        lax.fori_loop(0,cnt,gat,0)
        u=fs[0]-cx; v=fs[1]-cy; A=fs[2]; B=fs[3]; C=fs[4]; lo2=fs[5]
        p=A*u+B*v; r=B*u+C*v
        cf=[(-0.5*LOG2E)*A,(-LOG2E)*B,(-0.5*LOG2E)*C,LOG2E*p,LOG2E*r,(-0.5*LOG2E)*(u*p+v*r)+lo2,
            fs[6],fs[7],fs[8],fs[6],fs[7],fs[8],fs[6],fs[7],fs[8]]
        for k in range(15): xs[:,k,:]=cf[k]
        xs[:,15,:]=jnp.zeros_like(u)
        for c in range(3):
            ct=cot_ref[c:c+1,pl.ds(pl.multiple_of(ti*PIX,PIX),PIX)]
            h,m,l=split3(ct)
            for part in range(3):
                b=16*part+6+c
                rhs[b:b+1,PIX:]=h; rhs[b+3:b+4,PIX:]=m; rhs[b+6:b+7,PIX:]=l
        for c in range(3):
            cots[8*c:8*c+8,:]=jnp.broadcast_to(cot_ref[c:c+1,pl.ds(pl.multiple_of(ti*PIX,PIX),PIX)],(8,PIX))
        def slotp(tg,row0):
            for i in range(BU):
                x=xs[BU*tg+i]
                h,m,l=split3(x)
                y=jnp.concatenate([h,m,l,x,jnp.zeros((64,128),f32)],axis=0).T
                for k in range(8):
                    lhs[pl.ds(jnp.where(BU*tg+i<cnt,row0,4096),16,stride=8),:]=y[16*k:16*k+16,:]
                    row0=step_row(row0)
            return row0
        lax.fori_loop(0,(cnt+BU-1)//BU,slotp,0)
        rbs[...]=rhs[...].astype(bf16)
        def mm(b,h,dst):
            L=lhs[pl.ds(pl.multiple_of(b*128,128),128),0:48].astype(bf16)
            dst[...]=jnp.dot(L,rbs[:,h*PIX:h*PIX+PIX],preferred_element_type=f32)
        def fblock(b,src_):
            for jg in range(0,16,FJ):
                rows=[pl.ds(pl.multiple_of(b*128+8*jj,8),8) for jj in range(jg,jg+FJ)]
                cols=[]
                for rs in rows:
                    lrow=lhs[rs,:]
                    cols.append([jnp.broadcast_to(lrow[:,54+c:55+c],(8,128)) for c in range(3)])
                for i in range(8):
                    cs=slice(128*i,128*i+128)
                    T=st[0:8,cs]; I=[st[8+8*c:16+8*c,cs] for c in range(3)]
                    for m,rs in enumerate(rows):
                        aa=jnp.exp2(src_[8*(jg+m):8*(jg+m)+8,cs])
                        w=T*aa; T=T-w
                        for c in range(3): I[c]=I[c]+w*cols[m][c]
                        al[rs,cs]=aa; ws[rs,cs]=w
                    st[0:8,cs]=T
                    for c in range(3): st[8+8*c:16+8*c,cs]=I[c]
        st[0:8,:]=jnp.ones((8,PIX),f32)
        st[8:32,:]=jnp.zeros((24,PIX),f32)
        mm(0,0,eA)
        def fwd(b,_):
            nb=jnp.minimum(b+1,cnt-1)
            @pl.when(b%2==0)
            def _():
                mm(nb,0,eB); fblock(b,eA)
            @pl.when(b%2==1)
            def _():
                mm(nb,0,eA); fblock(b,eB)
            return 0
        lax.fori_loop(0,cnt,fwd,0)
        K=st[0:8,:]
        Cc=sum(st[8+8*c:16+8*c,:]*cots[8*c:8*c+8,:] for c in range(3))
        P=[jnp.ones((1,PIX),f32)]
        for s in range(7): P.append(P[-1]*K[s:s+1])
        V=[jnp.zeros((1,PIX),f32)]
        for s in range(7,0,-1): V.append(Cc[s:s+1]+K[s:s+1]*V[-1])
        Pv=jnp.concatenate(P,axis=0); V0=jnp.concatenate(V[::-1],axis=0)
        pref[...]=Pv
        lane128=lax.broadcasted_iota(jnp.int32,(8,128),1)//8
        def sums(sb_,zb_,r0):
            ra=jnp.dot(sb_[0:256],wa[...],preferred_element_type=f32)
            rc=jnp.dot(sb_[256:384],wb[...],preferred_element_type=f32)
            res[pl.ds(pl.multiple_of(r0,8),128),:]=ra[0:128]+ra[128:]+rc+zb_[...]
        def block(r0,qb,sb_,zb_):
            for jg in range(16-BJ,-1,-BJ):
                S=[[None]*3 for _ in range(BJ)]; Z=[[None]*3 for _ in range(BJ)]
                for i in range(7,-1,-1):
                    cs=slice(128*i,128*i+128)
                    V=vref[:,cs]; Pm=pref[:,cs]; ct=[cots[8*c:8*c+8,cs] for c in range(3)]
                    for m in range(BJ-1,-1,-1):
                        rs=pl.ds(pl.multiple_of(r0+8*(jg+m),8),8)
                        d=qb[8*(jg+m):8*(jg+m)+8,cs]-V
                        w=ws[rs,cs]*Pm
                        e=w*d
                        V=V+al[rs,cs]*d
                        for c in range(3):
                            zc=w*ct[c]
                            Z[m][c]=zc if i==7 else Z[m][c]+zc
                        s=S[m]
                        if i==7: s[0]=e; s[1]=e; s[2]=e
                        else:
                            s[0]=s[0]+e
                            if i>=1: s[1]=s[1]+s[0]; s[2]=s[2]+s[1]
                    vref[:,cs]=V
                for m in range(BJ):
                    zz=jnp.zeros((8,128),f32)
                    for c in range(3):
                        zz=jnp.where(lane128==6+c,jnp.sum(Z[m][c],axis=1,keepdims=True),zz)
                    zb_[8*(jg+m):8*(jg+m)+8,:]=zz
                for jp in range(0,BJ,2):
                    j=8*(jg+jp)
                    for m in range(3):
                        x=jnp.concatenate([S[jp][m],S[jp+1][m]],axis=0)
                        xh=x.astype(bf16); xl=(x-xh.astype(f32)).astype(bf16)
                        if m<2:
                            sb_[j:j+16,128*m:128*m+128]=xh
                            sb_[128+j:128+j+16,128*m:128*m+128]=xl
                        else:
                            sb_[256+j:256+j+16,0:128]=xh
                            sb_[256+j:256+j+16,128:256]=xl
        vref[...]=V0
        mm(cnt-1,1,eA)
        def bwd(i,_):
            b=cnt-1-i
            r0=pl.multiple_of(b*128,128)
            nb=jnp.maximum(b-1,0)
            @pl.when(i%2==0)
            def _():
                mm(nb,1,eB)
                sums(sbB,zbB,r0+128)
                block(r0,eA,sbA,zbA)
            @pl.when(i%2==1)
            def _():
                mm(nb,1,eA)
                sums(sbA,zbA,r0+128)
                block(r0,eB,sbB,zbB)
            return 0
        lax.fori_loop(0,cnt,bwd,0)
        @pl.when(cnt%2==1)
        def _(): sums(sbA,zbA,0)
        @pl.when(cnt%2==0)
        def _(): sums(sbB,zbB,0)
        sub=lax.broadcasted_iota(jnp.int32,(16,128),1)%8
        def slote(tg,row0):
            M=[None]*8
            for t in range(8):
                for k in range(8):
                    x=res[pl.ds(jnp.minimum(row0,last-1),16,stride=8),:]
                    M[k]=x if t==0 else jnp.where(sub==t,x,M[k])
                    row0=step_row(row0)
            Mt=jnp.concatenate(M,axis=0).T
            row=lambda k: Mt[8*k:8*k+8,:]
            mxx,mxy,myy,mx,my,m1=[row(k) for k in range(6)]
            tr=pl.ds(pl.multiple_of(8*tg,8),8)
            u=fs[0,tr,:]-cx; v=fs[1,tr,:]-cy; A=fs[2,tr,:]; B=fs[3,tr,:]; C=fs[4,tr,:]
            sx=mx-u*m1; sy=my-v*m1
            sxx=mxx-2.0*u*mx+u*u*m1
            syy=myy-2.0*v*my+v*v*m1
            sxy=mxy-u*my-v*mx+u*v*m1
            o=[A*sx+B*sy,B*sx+C*sy,-0.5*sxx,-sxy,-0.5*syy,m1]+[row(6+c) for c in range(3)]
            for t in range(8):
                @pl.when(8*tg+t<cnt)
                def _(t=t):
                    ow=blocks_ref[ti,8*tg+t]//16
                    for f in range(9): out_ref[ow,f]=o[f][t:t+1,:]
            return row0
        lax.fori_loop(0,(cnt+7)//8,slote,0)
        return 0
    lax.fori_loop(0,4,tile,0)
def tiles(blocks,counts,feat,cot):
    sm=pl.BlockSpec(memory_space=pltpu.SMEM); vm=pl.BlockSpec(memory_space=pltpu.VMEM)
    return pl.pallas_call(tiles_kernel,out_shape=jax.ShapeDtypeStruct((128,9,1,128),f32),
        in_specs=[sm,sm,vm,vm],out_specs=vm,
        scratch_shapes=[pltpu.VMEM((9,32,128),f32),pltpu.VMEM((32,16,128),f32),pltpu.VMEM((4096+128,128),f32),
            pltpu.VMEM((48,2*PIX),f32),pltpu.VMEM((256,128),bf16),pltpu.VMEM((256,128),bf16),pltpu.VMEM((8,PIX),f32),pltpu.VMEM((8,PIX),f32),
            pltpu.VMEM((32,PIX),f32),pltpu.VMEM((24,PIX),f32),pltpu.VMEM((48,2*PIX),bf16)]
            +[pltpu.VMEM((4096,PIX),f32)]*2+[pltpu.VMEM((128,PIX),f32)]*2
            +[pltpu.VMEM((384,256),bf16),pltpu.VMEM((128,128),f32)]*2+[pltpu.VMEM((4096+128,128),f32)],
        compiler_params=pltpu.CompilerParams(vmem_limit_bytes=67043328))(blocks,counts,feat,cot)


def load_params(p_ref):
    return [p_ref[row : row + 1, :].reshape(16, BLOCK) for row in range(59)]


def screen_rows(rows):
    return screen(rows, 1024.0, 512.0, 256.0)


def prep_kernel(idx_ref, p_ref, send_ref, fsc):
    for f, value in enumerate(screen_rows(load_params(p_ref))):
        fsc[f] = jnp.maximum(value, -1000.0) if f == 5 else value

    def put(d, _):
        for f in range(9):
            send_ref[d, f] = fsc[f, pl.ds(idx_ref[d], 1), :]
        return 0

    lax.fori_loop(0, 128, put, 0)


def final_kernel(idx_ref, p_ref, recv_ref, out_ref, acc):
    acc[...] = jnp.zeros_like(acc)

    def add(d, _):
        for f in range(9):
            acc[f, pl.ds(idx_ref[d], 1), :] = acc[f, pl.ds(idx_ref[d], 1), :] + recv_ref[d, f]
        return 0

    lax.fori_loop(0, 128, add, 0)
    pullback = jax.vjp(screen_rows, load_params(p_ref))[1]
    grads = [acc[f] for f in range(9)]
    grads[5] = grads[5] * (1.0 / LOG2E)
    for row, value in enumerate(pullback(grads)[0]):
        out_ref[row : row + 1, :] = value.reshape(1, 2048)


def exchange_kernel(x_ref, o_ref, ssem, rsem, lsem):
    n = lax.axis_size("dev")
    me = lax.axis_index("dev")
    bar = pltpu.get_barrier_semaphore()

    def sig(k, _):
        pl.semaphore_signal(bar, inc=1, device_id=(lax.rem(me + k, n),), device_id_type=pl.DeviceIdType.MESH)
        return 0

    lax.fori_loop(1, n, sig, 0)
    own = pltpu.make_async_copy(x_ref.at[me], o_ref.at[me], lsem)
    own.start()
    pl.semaphore_wait(bar, n - 1)

    def snd(k, _):
        peer = lax.rem(me + k, n)
        pltpu.make_async_remote_copy(
            src_ref=x_ref.at[peer],
            dst_ref=o_ref.at[me],
            send_sem=ssem,
            recv_sem=rsem,
            device_id=(peer,),
            device_id_type=pl.DeviceIdType.MESH,
        ).start()
        return 0

    lax.fori_loop(1, n, snd, 0)
    own.wait()
    most = pl.ds(0, n - 1)
    pltpu.make_async_copy(x_ref.at[most], x_ref.at[most], ssem).wait()
    pltpu.make_async_copy(o_ref.at[most], o_ref.at[most], rsem).wait()


def exchange(x, cid):
    vm = pl.BlockSpec(memory_space=pltpu.VMEM)
    return pl.pallas_call(
        exchange_kernel,
        out_shape=jax.ShapeDtypeStruct(x.shape, x.dtype),
        in_specs=[vm],
        out_specs=vm,
        scratch_shapes=[pltpu.SemaphoreType.DMA] * 3,
        compiler_params=pltpu.CompilerParams(collective_id=cid, has_side_effects=True),
    )(x)


def body(params, blocks, counts, pixel_grad):
    sm = pl.BlockSpec(memory_space=pltpu.SMEM)
    vm = pl.BlockSpec(memory_space=pltpu.VMEM)
    flat = blocks.reshape(-1)
    named = flat[:, None] // 16 == jnp.arange(128, dtype=jnp.int32)[None, :]
    want = jnp.sum(jnp.where(named, flat[:, None] % 16, 0), axis=0)
    asked = lax.all_to_all(want, "dev", 0, 0, tiled=True)
    send = pl.pallas_call(
        prep_kernel,
        out_shape=jax.ShapeDtypeStruct((128, 9, 1, 128), f32),
        in_specs=[sm, vm],
        out_specs=vm,
        scratch_shapes=[pltpu.VMEM((9, 16, 128), f32)],
    )(asked, params)
    feat = exchange(send, 0)
    grads = tiles(blocks, counts, feat, pixel_grad)
    back = exchange(grads, 1)
    return pl.pallas_call(
        final_kernel,
        out_shape=jax.ShapeDtypeStruct((59, 2048), f32),
        in_specs=[sm, vm, vm],
        out_specs=vm,
        scratch_shapes=[pltpu.VMEM((9, 16, 128), f32)],
    )(asked, params, back)


def solution(mesh):
    return jax.shard_map(
        body,
        mesh=mesh,
        in_specs=(P(None, "dev"), P("dev", None), P("dev"), P(None, "dev")),
        out_specs=P(None, "dev"),
        check_vma=False,
    )
```

```python
import jax
import jax.numpy as jnp
from jax import lax
from jax.experimental import pallas as pl
from jax.experimental.pallas import tpu as pltpu
from jax.sharding import PartitionSpec as P

LOG2E = 1.4426950408889634
sh_zero = 0.28209479177387814
sh_one = 0.4886025119029199
sh_two = [
    1.0925484305920792,
    -1.0925484305920792,
    0.31539156525252005,
    -1.0925484305920792,
    0.5462742152960396,
]
sh_three = [
    -0.5900435899266435,
    2.890611442640554,
    -0.4570457994644658,
    0.3731763325901154,
    -0.4570457994644658,
    1.445305721320277,
    -0.5900435899266435,
]


def sh_basis(dir_x, dir_y, dir_z):
    sq_x = dir_x * dir_x
    sq_y = dir_y * dir_y
    sq_z = dir_z * dir_z
    return [
        sh_zero + 0.0 * dir_x,
        -sh_one * dir_y,
        sh_one * dir_z,
        -sh_one * dir_x,
        sh_two[0] * dir_x * dir_y,
        sh_two[1] * dir_y * dir_z,
        sh_two[2] * (2.0 * sq_z - sq_x - sq_y),
        sh_two[3] * dir_x * dir_z,
        sh_two[4] * (sq_x - sq_y),
        sh_three[0] * dir_y * (3.0 * sq_x - sq_y),
        sh_three[1] * dir_x * dir_y * dir_z,
        sh_three[2] * dir_y * (4.0 * sq_z - sq_x - sq_y),
        sh_three[3] * dir_z * (2.0 * sq_z - 3.0 * sq_x - 3.0 * sq_y),
        sh_three[4] * dir_x * (4.0 * sq_z - sq_x - sq_y),
        sh_three[5] * dir_z * (sq_x - sq_y),
        sh_three[6] * dir_x * (sq_x - 3.0 * sq_y),
    ]


def screen(params, focal_len, centre_x, centre_y):
    mean_x, mean_y, depths = (params[0], params[1], params[2])
    scales = [jnp.exp(params[row]) for row in range(3, 6)]
    quat = params[6:10]
    norm = jnp.sqrt(quat[0] * quat[0] + quat[1] * quat[1] + quat[2] * quat[2] + quat[3] * quat[3])
    quat = [part / norm for part in quat]
    quat_r, quat_i, quat_j, quat_k = (quat[0], quat[1], quat[2], quat[3])
    rotation = [
        [
            1.0 - 2.0 * (quat_j * quat_j + quat_k * quat_k),
            2.0 * (quat_i * quat_j - quat_r * quat_k),
            2.0 * (quat_i * quat_k + quat_r * quat_j),
        ],
        [
            2.0 * (quat_i * quat_j + quat_r * quat_k),
            1.0 - 2.0 * (quat_i * quat_i + quat_k * quat_k),
            2.0 * (quat_j * quat_k - quat_r * quat_i),
        ],
        [
            2.0 * (quat_i * quat_k - quat_r * quat_j),
            2.0 * (quat_j * quat_k + quat_r * quat_i),
            1.0 - 2.0 * (quat_i * quat_i + quat_j * quat_j),
        ],
    ]
    inv_z = 1.0 / depths
    diag_jac = focal_len * inv_z
    side_x = -focal_len * mean_x * inv_z * inv_z
    side_y = -focal_len * mean_y * inv_z * inv_z
    upper = [
        (diag_jac * rotation[0][column] + side_x * rotation[2][column]) * scales[column]
        for column in range(3)
    ]
    lower = [
        (diag_jac * rotation[1][column] + side_y * rotation[2][column]) * scales[column]
        for column in range(3)
    ]
    cov_xx = upper[0] * upper[0] + upper[1] * upper[1] + upper[2] * upper[2] + 0.3
    cov_xy = upper[0] * lower[0] + upper[1] * lower[1] + upper[2] * lower[2]
    cov_yy = lower[0] * lower[0] + lower[1] * lower[1] + lower[2] * lower[2] + 0.3
    determ = cov_xx * cov_yy - cov_xy * cov_xy
    screen_u = focal_len * mean_x * inv_z + centre_x
    screen_v = focal_len * mean_y * inv_z + centre_y
    logit = params[10]
    log_opacity = (logit - jnp.log1p(jnp.exp(logit))) * LOG2E
    distance = jnp.sqrt(mean_x * mean_x + mean_y * mean_y + depths * depths)
    basis = sh_basis(mean_x / distance, mean_y / distance, depths / distance)
    colors = [
        0.5
        + sum((basis[harmonic] * params[11 + 16 * channel + harmonic] for harmonic in range(16)))
        for channel in range(3)
    ]
    return [screen_u, screen_v, cov_yy / determ, -cov_xy / determ, cov_xx / determ, log_opacity] + colors
BLOCK=128; SIDE=32; TX=32; PIX=1024; MAXB=32
BU=4; FJ=4; BJ=4
f32=jnp.float32; bf16=jnp.bfloat16

def split3(x):
    hi=x.astype(bf16).astype(f32); r=x-hi
    mid=r.astype(bf16).astype(f32); lo=r-mid
    return hi,mid,lo

def tiles_kernel(ints_ref, feat2_ref, cot2_ref, out2_ref,
                 fs, xs, lhs, rhs, wa, wb, pref, vref, st, cots, rbs, al, ws, eA, eB, sbA, zbA, sbB, zbB, res):
    me=lax.axis_index("dev")
    odd=me%2
    mine=[ints_ref[1,0,k] for k in range(4)]; other=[ints_ref[3,0,k] for k in range(4)]
    sm_,so_=sum(mine),sum(other)
    own_full=jnp.logical_or(sm_>so_,jnp.logical_and(sm_==so_,odd==0))
    full=[jnp.where(own_full,a,b) for a,b in zip(mine,other)]
    hi_=jnp.maximum(sm_,so_); lo_=jnp.minimum(sm_,so_)
    best,pick=hi_,jnp.int32(0)
    for sub in range(1,15):
        moved=sum(full[k] for k in range(4) if sub>>k&1)
        top=jnp.maximum(hi_-moved,lo_+moved)
        better=top<best
        pick=jnp.where(better,sub,pick); best=jnp.where(better,top,best)
    lane=lax.broadcasted_iota(jnp.int32,(1,PIX),1)
    X=(lane%SIDE-16).astype(f32); Y=(lane//SIDE-16).astype(f32)
    mono=[X*X,X*Y,Y*Y,X,Y,jnp.ones_like(X)]
    out2_ref[...]=jnp.zeros_like(out2_ref)
    rhs[...]=jnp.zeros_like(rhs)
    for part in range(3):
        for k in range(6): rhs[16*part+k:16*part+k+1,0:PIX]=mono[k]
    x1=X[:,0:128]; y1=(lax.broadcasted_iota(jnp.int32,(1,128),1)//SIDE-16).astype(f32); o1=jnp.ones_like(x1); z1=jnp.zeros_like(x1)
    pad=jnp.zeros((80,128),f32)
    rep=lambda rows: jnp.concatenate([jnp.broadcast_to(x,(8,128)) for x in rows]+[pad],axis=0).T
    W0=rep([x1*x1,x1*y1,y1*y1,x1,y1,o1])
    W1=rep([z1,4.0*x1,8.0*y1-16.0,z1,4.0*o1,z1])
    W2=rep([z1,z1,32.0*o1,z1,z1,z1])
    wa[...]=jnp.concatenate([W0,W1],axis=0).astype(bf16)
    wb[...]=jnp.concatenate([W2,W2],axis=0).astype(bf16)
    def tile(tx,_):
        who=tx//4; ti=tx%4
        gone=jnp.bitwise_and(jnp.right_shift(pick,ti),1)
        here=jnp.where(own_full,jnp.logical_and(who==0,gone==0),jnp.logical_or(who==0,gone==1))
        @pl.when(here)
        def _():
            one_tile(who,ti)
        return 0
    def one_tile(who,ti):
        feat_ref=feat2_ref.at[who]; cot_ref=cot2_ref.at[who]; out_ref=out2_ref.at[who]
        cnt=ints_ref[2*who+1,0,ti]
        tid=jnp.where(who==0,me,me+1-2*odd)*4+ti
        cx=((tid%TX)*SIDE).astype(f32)+16.5
        cy=((tid//TX)*SIDE).astype(f32)+16.5
        last=128*cnt
        def step_row(r):
            r=r+128
            return jnp.where(r>=last,r-last+1,r)
        def gat(t,_):
            ow=ints_ref[2*who,0,ti*32+t]//16
            for f in range(9): fs[f,pl.ds(t,1),:]=feat_ref[ow,f]
            return 0
        lax.fori_loop(0,cnt,gat,0)
        u=fs[0]-cx; v=fs[1]-cy; A=fs[2]; B=fs[3]; C=fs[4]; lo2=fs[5]
        p=A*u+B*v; r=B*u+C*v
        cf=[(-0.5*LOG2E)*A,(-LOG2E)*B,(-0.5*LOG2E)*C,LOG2E*p,LOG2E*r,(-0.5*LOG2E)*(u*p+v*r)+lo2,
            fs[6],fs[7],fs[8],fs[6],fs[7],fs[8],fs[6],fs[7],fs[8]]
        for k in range(15): xs[:,k,:]=cf[k]
        xs[:,15,:]=jnp.zeros_like(u)
        for c in range(3):
            ct=cot_ref[c:c+1,pl.ds(pl.multiple_of(ti*PIX,PIX),PIX)]
            h,m,l=split3(ct)
            for part in range(3):
                b=16*part+6+c
                rhs[b:b+1,PIX:]=h; rhs[b+3:b+4,PIX:]=m; rhs[b+6:b+7,PIX:]=l
        for c in range(3):
            cots[8*c:8*c+8,:]=jnp.broadcast_to(cot_ref[c:c+1,pl.ds(pl.multiple_of(ti*PIX,PIX),PIX)],(8,PIX))
        def slotp(tg,row0):
            for i in range(BU):
                x=xs[BU*tg+i]
                h,m,l=split3(x)
                y=jnp.concatenate([h,m,l,x,jnp.zeros((64,128),f32)],axis=0).T
                for k in range(8):
                    lhs[pl.ds(jnp.where(BU*tg+i<cnt,row0,4096),16,stride=8),:]=y[16*k:16*k+16,:]
                    row0=step_row(row0)
            return row0
        lax.fori_loop(0,(cnt+BU-1)//BU,slotp,0)
        rbs[...]=rhs[...].astype(bf16)
        def mm(b,h,dst):
            L=lhs[pl.ds(pl.multiple_of(b*128,128),128),0:48].astype(bf16)
            dst[...]=jnp.dot(L,rbs[:,h*PIX:h*PIX+PIX],preferred_element_type=f32)
        def fblock(b,src_):
            for jg in range(0,16,FJ):
                rows=[pl.ds(pl.multiple_of(b*128+8*jj,8),8) for jj in range(jg,jg+FJ)]
                cols=[]
                for rs in rows:
                    lrow=lhs[rs,:]
                    cols.append([jnp.broadcast_to(lrow[:,54+c:55+c],(8,128)) for c in range(3)])
                for i in range(8):
                    cs=slice(128*i,128*i+128)
                    T=st[0:8,cs]; I=[st[8+8*c:16+8*c,cs] for c in range(3)]
                    for m,rs in enumerate(rows):
                        aa=jnp.exp2(src_[8*(jg+m):8*(jg+m)+8,cs])
                        w=T*aa; T=T-w
                        for c in range(3): I[c]=I[c]+w*cols[m][c]
                        al[rs,cs]=aa; ws[rs,cs]=w
                    st[0:8,cs]=T
                    for c in range(3): st[8+8*c:16+8*c,cs]=I[c]
        st[0:8,:]=jnp.ones((8,PIX),f32)
        st[8:32,:]=jnp.zeros((24,PIX),f32)
        mm(0,0,eA)
        def fwd(b,_):
            nb=jnp.minimum(b+1,cnt-1)
            @pl.when(b%2==0)
            def _():
                mm(nb,0,eB); fblock(b,eA)
            @pl.when(b%2==1)
            def _():
                mm(nb,0,eA); fblock(b,eB)
            return 0
        lax.fori_loop(0,cnt,fwd,0)
        K=st[0:8,:]
        Cc=sum(st[8+8*c:16+8*c,:]*cots[8*c:8*c+8,:] for c in range(3))
        P=[jnp.ones((1,PIX),f32)]
        for s in range(7): P.append(P[-1]*K[s:s+1])
        V=[jnp.zeros((1,PIX),f32)]
        for s in range(7,0,-1): V.append(Cc[s:s+1]+K[s:s+1]*V[-1])
        Pv=jnp.concatenate(P,axis=0); V0=jnp.concatenate(V[::-1],axis=0)
        pref[...]=Pv
        lane128=lax.broadcasted_iota(jnp.int32,(8,128),1)//8
        def sums(sb_,zb_,r0):
            ra=jnp.dot(sb_[0:256],wa[...],preferred_element_type=f32)
            rc=jnp.dot(sb_[256:384],wb[...],preferred_element_type=f32)
            res[pl.ds(pl.multiple_of(r0,8),128),:]=ra[0:128]+ra[128:]+rc+zb_[...]
        def block(r0,qb,sb_,zb_):
            for jg in range(16-BJ,-1,-BJ):
                S=[[None]*3 for _ in range(BJ)]; Z=[[None]*3 for _ in range(BJ)]
                for i in range(7,-1,-1):
                    cs=slice(128*i,128*i+128)
                    V=vref[:,cs]; Pm=pref[:,cs]; ct=[cots[8*c:8*c+8,cs] for c in range(3)]
                    for m in range(BJ-1,-1,-1):
                        rs=pl.ds(pl.multiple_of(r0+8*(jg+m),8),8)
                        d=qb[8*(jg+m):8*(jg+m)+8,cs]-V
                        w=ws[rs,cs]*Pm
                        e=w*d
                        V=V+al[rs,cs]*d
                        for c in range(3):
                            zc=w*ct[c]
                            Z[m][c]=zc if i==7 else Z[m][c]+zc
                        s=S[m]
                        if i==7: s[0]=e; s[1]=e; s[2]=e
                        else:
                            s[0]=s[0]+e
                            if i>=1: s[1]=s[1]+s[0]; s[2]=s[2]+s[1]
                    vref[:,cs]=V
                for m in range(BJ):
                    zz=jnp.zeros((8,128),f32)
                    for c in range(3):
                        zz=jnp.where(lane128==6+c,jnp.sum(Z[m][c],axis=1,keepdims=True),zz)
                    zb_[8*(jg+m):8*(jg+m)+8,:]=zz
                for jp in range(0,BJ,2):
                    j=8*(jg+jp)
                    for m in range(3):
                        x=jnp.concatenate([S[jp][m],S[jp+1][m]],axis=0)
                        xh=x.astype(bf16); xl=(x-xh.astype(f32)).astype(bf16)
                        if m<2:
                            sb_[j:j+16,128*m:128*m+128]=xh
                            sb_[128+j:128+j+16,128*m:128*m+128]=xl
                        else:
                            sb_[256+j:256+j+16,0:128]=xh
                            sb_[256+j:256+j+16,128:256]=xl
        vref[...]=V0
        mm(cnt-1,1,eA)
        def bwd(i,_):
            b=cnt-1-i
            r0=pl.multiple_of(b*128,128)
            nb=jnp.maximum(b-1,0)
            @pl.when(i%2==0)
            def _():
                mm(nb,1,eB)
                sums(sbB,zbB,r0+128)
                block(r0,eA,sbA,zbA)
            @pl.when(i%2==1)
            def _():
                mm(nb,1,eA)
                sums(sbA,zbA,r0+128)
                block(r0,eB,sbB,zbB)
            return 0
        lax.fori_loop(0,cnt,bwd,0)
        @pl.when(cnt%2==1)
        def _(): sums(sbA,zbA,0)
        @pl.when(cnt%2==0)
        def _(): sums(sbB,zbB,0)
        sub=lax.broadcasted_iota(jnp.int32,(16,128),1)%8
        def slote(tg,row0):
            M=[None]*8
            for t in range(8):
                for k in range(8):
                    x=res[pl.ds(jnp.minimum(row0,last-1),16,stride=8),:]
                    M[k]=x if t==0 else jnp.where(sub==t,x,M[k])
                    row0=step_row(row0)
            Mt=jnp.concatenate(M,axis=0).T
            row=lambda k: Mt[8*k:8*k+8,:]
            mxx,mxy,myy,mx,my,m1=[row(k) for k in range(6)]
            tr=pl.ds(pl.multiple_of(8*tg,8),8)
            u=fs[0,tr,:]-cx; v=fs[1,tr,:]-cy; A=fs[2,tr,:]; B=fs[3,tr,:]; C=fs[4,tr,:]
            sx=mx-u*m1; sy=my-v*m1
            sxx=mxx-2.0*u*mx+u*u*m1
            syy=myy-2.0*v*my+v*v*m1
            sxy=mxy-u*my-v*mx+u*v*m1
            o=[A*sx+B*sy,B*sx+C*sy,-0.5*sxx,-sxy,-0.5*syy,m1]+[row(6+c) for c in range(3)]
            for t in range(8):
                @pl.when(8*tg+t<cnt)
                def _(t=t):
                    ow=ints_ref[2*who,0,ti*32+8*tg+t]//16
                    for f in range(9): out_ref[ow,f]=o[f][t:t+1,:]
            return row0
        lax.fori_loop(0,(cnt+7)//8,slote,0)
        return 0
    lax.fori_loop(0,8,tile,0)
def tiles(ints,feat,cot):
    sm=pl.BlockSpec(memory_space=pltpu.SMEM); vm=pl.BlockSpec(memory_space=pltpu.VMEM)
    return pl.pallas_call(tiles_kernel,out_shape=jax.ShapeDtypeStruct((2,128,9,1,128),f32),
        in_specs=[sm,vm,vm],out_specs=vm,
        scratch_shapes=[pltpu.VMEM((9,32,128),f32),pltpu.VMEM((32,16,128),f32),pltpu.VMEM((4096+128,128),f32),
            pltpu.VMEM((48,2*PIX),f32),pltpu.VMEM((256,128),bf16),pltpu.VMEM((256,128),bf16),pltpu.VMEM((8,PIX),f32),pltpu.VMEM((8,PIX),f32),
            pltpu.VMEM((32,PIX),f32),pltpu.VMEM((24,PIX),f32),pltpu.VMEM((48,2*PIX),bf16)]
            +[pltpu.VMEM((4096,PIX),f32)]*2+[pltpu.VMEM((128,PIX),f32)]*2
            +[pltpu.VMEM((384,256),bf16),pltpu.VMEM((128,128),f32)]*2+[pltpu.VMEM((4096+128,128),f32)],
        compiler_params=pltpu.CompilerParams(vmem_limit_bytes=67043328))(ints,feat,cot)


def load_params(p_ref):
    return [p_ref[row : row + 1, :].reshape(16, BLOCK) for row in range(59)]


def screen_rows(rows):
    return screen(rows, 1024.0, 512.0, 256.0)


def everyone(me, n, act):
    def step(k, _):
        act(lax.rem(me + k, n))
        return 0

    lax.fori_loop(1, n, step, 0)


def send(src, dst, ssem, rsem, peer):
    return pltpu.make_async_remote_copy(
        src_ref=src,
        dst_ref=dst,
        send_sem=ssem,
        recv_sem=rsem,
        device_id=(peer,),
        device_id_type=pl.DeviceIdType.MESH,
    )


def all_but_one(ref, sem):
    rest = ref.at[pl.ds(0, ref.shape[0] - 1)]
    return pltpu.make_async_copy(rest, rest, sem)


def greet(me, n):
    bar = pltpu.get_barrier_semaphore()
    everyone(
        me,
        n,
        lambda peer: pl.semaphore_signal(bar, inc=1, device_id=(peer,), device_id_type=pl.DeviceIdType.MESH),
    )
    return bar


def forward_kernel(ints_ref, p_ref, cot_ref, pair_ref, feat_ref, cot2_ref, idx_ref, lists, fsc, outbox, idxs, sems):
    n = lax.axis_size("dev")
    me = lax.axis_index("dev")
    partner = me + 1 - 2 * lax.rem(me, 2)
    bar = greet(me, n)
    own_list = pltpu.make_async_copy(ints_ref.at[0], lists.at[me], sems.at[0])
    own_ints = pltpu.make_async_copy(ints_ref, pair_ref.at[pl.ds(0, 2)], sems.at[1])
    own_cot = pltpu.make_async_copy(cot_ref, cot2_ref.at[0], sems.at[2])
    own_list.start()
    own_ints.start()
    own_cot.start()
    for f, value in enumerate(screen_rows(load_params(p_ref))):
        fsc[f] = jnp.maximum(value, -1000.0) if f == 5 else value
    pl.semaphore_wait(bar, n - 1)
    everyone(me, n, lambda peer: send(ints_ref.at[0], lists.at[me], sems.at[3], sems.at[4], peer).start())
    pair_ints = send(ints_ref, pair_ref.at[pl.ds(2, 2)], sems.at[5], sems.at[6], partner)
    pair_cot = send(cot_ref, cot2_ref.at[1], sems.at[7], sems.at[8], partner)
    pair_ints.start()
    pair_cot.start()
    own_list.wait()
    all_but_one(lists, sems.at[4]).wait()
    flat = lists[...].reshape(128, 128)
    asked = jnp.sum(jnp.where(flat >> 4 == me, flat & 15, 0).astype(f32), axis=1, keepdims=True)
    idx_ref[...] = jnp.broadcast_to(asked, (128, 128)).T[0:1].astype(jnp.int32)
    to_scalar = pltpu.make_async_copy(idx_ref, idxs, sems.at[9])
    to_scalar.start()
    to_scalar.wait()

    def put(d, _):
        for f in range(9):
            outbox[d, f] = fsc[f, pl.ds(idxs[0, d] & 15, 1), :]
        return 0

    lax.fori_loop(0, 128, put, 0)
    own_feat = pltpu.make_async_copy(outbox.at[me], feat_ref.at[0, me], sems.at[10])
    own_feat.start()
    everyone(me, n, lambda peer: send(outbox.at[peer], feat_ref.at[0, me], sems.at[11], sems.at[12], peer).start())
    all_but_one(lists, sems.at[3]).wait()
    own_ints.wait()
    own_cot.wait()
    own_feat.wait()
    pair_ints.wait()
    pair_cot.wait()
    all_but_one(outbox, sems.at[12]).wait()
    pair_feat = send(feat_ref.at[0], feat_ref.at[1], sems.at[13], sems.at[14], partner)
    pair_feat.start()
    all_but_one(outbox, sems.at[11]).wait()
    pair_feat.wait()


def back_kernel(grad_ref, recv_ref, theirs, outbox, sems):
    n = lax.axis_size("dev")
    me = lax.axis_index("dev")
    partner = me + 1 - 2 * lax.rem(me, 2)
    bar = greet(me, n)
    pl.semaphore_wait(bar, n - 1)
    pair = send(grad_ref.at[1], theirs, sems.at[0], sems.at[1], partner)
    pair.start()
    pair.wait_recv()

    def add(d, _):
        for f in range(9):
            outbox[d, f] = grad_ref[0, d, f] + theirs[d, f]
        return 0

    lax.fori_loop(0, 128, add, 0)
    own = pltpu.make_async_copy(outbox.at[me], recv_ref.at[me], sems.at[2])
    own.start()
    everyone(me, n, lambda peer: send(outbox.at[peer], recv_ref.at[me], sems.at[3], sems.at[4], peer).start())
    pair.wait_send()
    own.wait()
    all_but_one(outbox, sems.at[3]).wait()
    all_but_one(recv_ref, sems.at[4]).wait()


def final_kernel(idx_ref, p_ref, recv_ref, out_ref):
    rows = lax.broadcasted_iota(jnp.int32, (16, BLOCK), 0)

    def add(d, acc):
        hit = rows == idx_ref[0, d]
        return tuple(
            acc[f] + jnp.where(hit, jnp.broadcast_to(recv_ref[d, f], (16, BLOCK)), 0.0) for f in range(9)
        )

    zeros = tuple(jnp.zeros((16, BLOCK), f32) for _ in range(9))
    grads = list(lax.fori_loop(0, 128, add, zeros, unroll=4))
    pullback = jax.vjp(screen_rows, load_params(p_ref))[1]
    grads[5] = grads[5] * (1.0 / LOG2E)
    for row, value in enumerate(pullback(grads)[0]):
        out_ref[row : row + 1, :] = value.reshape(1, 2048)


def body(params, blocks, counts, pixel_grad):
    sm = pl.BlockSpec(memory_space=pltpu.SMEM)
    vm = pl.BlockSpec(memory_space=pltpu.VMEM)
    block_sums = jax.ShapeDtypeStruct((128, 9, 1, 128), f32)
    ints = jnp.stack([blocks.reshape(1, 128), jnp.pad(counts, (0, 124)).reshape(1, 128)])
    pair, feat, cot, idx = pl.pallas_call(
        forward_kernel,
        out_shape=[
            jax.ShapeDtypeStruct((4, 1, 128), jnp.int32),
            jax.ShapeDtypeStruct((2, 128, 9, 1, 128), f32),
            jax.ShapeDtypeStruct((2, 3, 4096), f32),
            jax.ShapeDtypeStruct((1, 128), jnp.int32),
        ],
        in_specs=[vm, vm, vm],
        out_specs=[vm, vm, vm, vm],
        scratch_shapes=[
            pltpu.VMEM((128, 1, 128), jnp.int32),
            pltpu.VMEM((9, 16, 128), f32),
            pltpu.VMEM((128, 9, 1, 128), f32),
            pltpu.SMEM((1, 128), jnp.int32),
            pltpu.SemaphoreType.DMA((15,)),
        ],
        compiler_params=pltpu.CompilerParams(collective_id=0, has_side_effects=True),
    )(ints, params, pixel_grad)
    grads = tiles(pair, feat, cot)
    back = pl.pallas_call(
        back_kernel,
        out_shape=block_sums,
        in_specs=[vm],
        out_specs=vm,
        scratch_shapes=[
            pltpu.VMEM((128, 9, 1, 128), f32),
            pltpu.VMEM((128, 9, 1, 128), f32),
            pltpu.SemaphoreType.DMA((5,)),
        ],
        compiler_params=pltpu.CompilerParams(collective_id=1, has_side_effects=True),
    )(grads)
    return pl.pallas_call(
        final_kernel,
        out_shape=jax.ShapeDtypeStruct((59, 2048), f32),
        in_specs=[sm, vm, vm],
        out_specs=vm,
    )(idx, params, back)


def solution(mesh):
    return jax.shard_map(
        body,
        mesh=mesh,
        in_specs=(P(None, "dev"), P("dev", None), P("dev"), P(None, "dev")),
        out_specs=P(None, "dev"),
        check_vma=False,
    )
```

```python
import jax
import jax.numpy as jnp
from jax import lax
from jax.experimental import pallas as pl
from jax.experimental.pallas import tpu as pltpu
from jax.sharding import PartitionSpec as P

LOG2E = 1.4426950408889634
sh_zero = 0.28209479177387814
sh_one = 0.4886025119029199
sh_two = [
    1.0925484305920792,
    -1.0925484305920792,
    0.31539156525252005,
    -1.0925484305920792,
    0.5462742152960396,
]
sh_three = [
    -0.5900435899266435,
    2.890611442640554,
    -0.4570457994644658,
    0.3731763325901154,
    -0.4570457994644658,
    1.445305721320277,
    -0.5900435899266435,
]


def sh_basis(dir_x, dir_y, dir_z):
    sq_x = dir_x * dir_x
    sq_y = dir_y * dir_y
    sq_z = dir_z * dir_z
    return [
        sh_zero + 0.0 * dir_x,
        -sh_one * dir_y,
        sh_one * dir_z,
        -sh_one * dir_x,
        sh_two[0] * dir_x * dir_y,
        sh_two[1] * dir_y * dir_z,
        sh_two[2] * (2.0 * sq_z - sq_x - sq_y),
        sh_two[3] * dir_x * dir_z,
        sh_two[4] * (sq_x - sq_y),
        sh_three[0] * dir_y * (3.0 * sq_x - sq_y),
        sh_three[1] * dir_x * dir_y * dir_z,
        sh_three[2] * dir_y * (4.0 * sq_z - sq_x - sq_y),
        sh_three[3] * dir_z * (2.0 * sq_z - 3.0 * sq_x - 3.0 * sq_y),
        sh_three[4] * dir_x * (4.0 * sq_z - sq_x - sq_y),
        sh_three[5] * dir_z * (sq_x - sq_y),
        sh_three[6] * dir_x * (sq_x - 3.0 * sq_y),
    ]


def screen(params, focal_len, centre_x, centre_y):
    mean_x, mean_y, depths = (params[0], params[1], params[2])
    scales = [jnp.exp(params[row]) for row in range(3, 6)]
    quat = params[6:10]
    norm = jnp.sqrt(quat[0] * quat[0] + quat[1] * quat[1] + quat[2] * quat[2] + quat[3] * quat[3])
    quat = [part / norm for part in quat]
    quat_r, quat_i, quat_j, quat_k = (quat[0], quat[1], quat[2], quat[3])
    rotation = [
        [
            1.0 - 2.0 * (quat_j * quat_j + quat_k * quat_k),
            2.0 * (quat_i * quat_j - quat_r * quat_k),
            2.0 * (quat_i * quat_k + quat_r * quat_j),
        ],
        [
            2.0 * (quat_i * quat_j + quat_r * quat_k),
            1.0 - 2.0 * (quat_i * quat_i + quat_k * quat_k),
            2.0 * (quat_j * quat_k - quat_r * quat_i),
        ],
        [
            2.0 * (quat_i * quat_k - quat_r * quat_j),
            2.0 * (quat_j * quat_k + quat_r * quat_i),
            1.0 - 2.0 * (quat_i * quat_i + quat_j * quat_j),
        ],
    ]
    inv_z = 1.0 / depths
    diag_jac = focal_len * inv_z
    side_x = -focal_len * mean_x * inv_z * inv_z
    side_y = -focal_len * mean_y * inv_z * inv_z
    upper = [
        (diag_jac * rotation[0][column] + side_x * rotation[2][column]) * scales[column]
        for column in range(3)
    ]
    lower = [
        (diag_jac * rotation[1][column] + side_y * rotation[2][column]) * scales[column]
        for column in range(3)
    ]
    cov_xx = upper[0] * upper[0] + upper[1] * upper[1] + upper[2] * upper[2] + 0.3
    cov_xy = upper[0] * lower[0] + upper[1] * lower[1] + upper[2] * lower[2]
    cov_yy = lower[0] * lower[0] + lower[1] * lower[1] + lower[2] * lower[2] + 0.3
    determ = cov_xx * cov_yy - cov_xy * cov_xy
    screen_u = focal_len * mean_x * inv_z + centre_x
    screen_v = focal_len * mean_y * inv_z + centre_y
    logit = params[10]
    log_opacity = (logit - jnp.log1p(jnp.exp(logit))) * LOG2E
    distance = jnp.sqrt(mean_x * mean_x + mean_y * mean_y + depths * depths)
    basis = sh_basis(mean_x / distance, mean_y / distance, depths / distance)
    colors = [
        0.5
        + sum((basis[harmonic] * params[11 + 16 * channel + harmonic] for harmonic in range(16)))
        for channel in range(3)
    ]
    return [screen_u, screen_v, cov_yy / determ, -cov_xy / determ, cov_xx / determ, log_opacity] + colors
BLOCK=128; SIDE=32; TX=32; PIX=1024; MAXB=32
BU=4; FJ=1; BJ=2
f32=jnp.float32; bf16=jnp.bfloat16

def split3(x):
    hi=x.astype(bf16).astype(f32); r=x-hi
    mid=r.astype(bf16).astype(f32); lo=r-mid
    return hi,mid,lo

def tiles_kernel(ints_ref, feat2_ref, cot2_ref, out2_ref,
                 fs, xs, lhs, rhs, wa, wb, pref, vref, st, cots, rbs, al, ws, eA, eB, sbA, zbA, sbB, zbB, res):
    me=lax.axis_index("dev")
    odd=me%2
    mine=[ints_ref[1,0,k] for k in range(4)]; other=[ints_ref[3,0,k] for k in range(4)]
    sm_,so_=sum(mine),sum(other)
    own_full=jnp.logical_or(sm_>so_,jnp.logical_and(sm_==so_,odd==0))
    full=[jnp.where(own_full,a,b) for a,b in zip(mine,other)]
    hi_=jnp.maximum(sm_,so_); lo_=jnp.minimum(sm_,so_)
    best,pick=hi_,jnp.int32(0)
    for sub in range(1,15):
        moved=sum(full[k] for k in range(4) if sub>>k&1)
        top=jnp.maximum(hi_-moved,lo_+moved)
        better=top<best
        pick=jnp.where(better,sub,pick); best=jnp.where(better,top,best)
    lane=lax.broadcasted_iota(jnp.int32,(1,PIX),1)
    X=(lane%SIDE-16).astype(f32); Y=(lane//SIDE-16).astype(f32)
    mono=[X*X,X*Y,Y*Y,X,Y,jnp.ones_like(X)]
    out2_ref[...]=jnp.zeros_like(out2_ref)
    rhs[...]=jnp.zeros_like(rhs)
    for part in range(3):
        for k in range(6): rhs[16*part+k:16*part+k+1,0:PIX]=mono[k]
    x1=X[:,0:128]; y1=(lax.broadcasted_iota(jnp.int32,(1,128),1)//SIDE-16).astype(f32); o1=jnp.ones_like(x1); z1=jnp.zeros_like(x1)
    pad=jnp.zeros((80,128),f32)
    rep=lambda rows: jnp.concatenate([jnp.broadcast_to(x,(8,128)) for x in rows]+[pad],axis=0).T
    W0=rep([x1*x1,x1*y1,y1*y1,x1,y1,o1])
    W1=rep([z1,4.0*x1,8.0*y1-16.0,z1,4.0*o1,z1])
    W2=rep([z1,z1,32.0*o1,z1,z1,z1])
    wa[...]=jnp.concatenate([W0,W1],axis=0).astype(bf16)
    wb[...]=jnp.concatenate([W2,W2],axis=0).astype(bf16)
    def tile(tx,_):
        who=tx//4; ti=tx%4
        gone=jnp.bitwise_and(jnp.right_shift(pick,ti),1)
        here=jnp.where(own_full,jnp.logical_and(who==0,gone==0),jnp.logical_or(who==0,gone==1))
        @pl.when(here)
        def _():
            one_tile(who,ti)
        return 0
    def one_tile(who,ti):
        feat_ref=feat2_ref.at[who]; cot_ref=cot2_ref.at[who]; out_ref=out2_ref.at[who]
        cnt=ints_ref[2*who+1,0,ti]
        tid=jnp.where(who==0,me,me+1-2*odd)*4+ti
        cx=((tid%TX)*SIDE).astype(f32)+16.5
        cy=((tid//TX)*SIDE).astype(f32)+16.5
        last=128*cnt
        def step_row(r):
            r=r+128
            return jnp.where(r>=last,r-last+1,r)
        def gat(t,_):
            ow=ints_ref[2*who,0,ti*32+t]//16
            for f in range(9): fs[f,pl.ds(t,1),:]=feat_ref[ow,f]
            return 0
        lax.fori_loop(0,cnt,gat,0)
        u=fs[0]-cx; v=fs[1]-cy; A=fs[2]; B=fs[3]; C=fs[4]; lo2=fs[5]
        p=A*u+B*v; r=B*u+C*v
        cf=[(-0.5*LOG2E)*A,(-LOG2E)*B,(-0.5*LOG2E)*C,LOG2E*p,LOG2E*r,(-0.5*LOG2E)*(u*p+v*r)+lo2,
            fs[6],fs[7],fs[8],fs[6],fs[7],fs[8],fs[6],fs[7],fs[8]]
        for k in range(15): xs[:,k,:]=cf[k]
        xs[:,15,:]=jnp.zeros_like(u)
        for c in range(3):
            ct=cot_ref[c:c+1,pl.ds(pl.multiple_of(ti*PIX,PIX),PIX)]
            h,m,l=split3(ct)
            for part in range(3):
                b=16*part+6+c
                rhs[b:b+1,PIX:]=h; rhs[b+3:b+4,PIX:]=m; rhs[b+6:b+7,PIX:]=l
        for c in range(3):
            cots[8*c:8*c+8,:]=jnp.broadcast_to(cot_ref[c:c+1,pl.ds(pl.multiple_of(ti*PIX,PIX),PIX)],(8,PIX))
        def slotp(tg,row0):
            for i in range(BU):
                x=xs[BU*tg+i]
                h,m,l=split3(x)
                y=jnp.concatenate([h,m,l,x,jnp.zeros((64,128),f32)],axis=0).T
                for k in range(8):
                    lhs[pl.ds(jnp.where(BU*tg+i<cnt,row0,4096),16,stride=8),:]=y[16*k:16*k+16,:]
                    row0=step_row(row0)
            return row0
        lax.fori_loop(0,(cnt+BU-1)//BU,slotp,0)
        rbs[...]=rhs[...].astype(bf16)
        def mm(b,h,dst):
            L=lhs[pl.ds(pl.multiple_of(b*128,128),128),0:48].astype(bf16)
            dst[...]=jnp.dot(L,rbs[:,h*PIX:h*PIX+PIX],preferred_element_type=f32)
        def fblock(b,src_):
            for jg in range(0,16,FJ):
                rows=[pl.ds(pl.multiple_of(b*128+8*jj,8),8) for jj in range(jg,jg+FJ)]
                cols=[]
                for rs in rows:
                    lrow=lhs[rs,:]
                    cols.append([jnp.broadcast_to(lrow[:,54+c:55+c],(8,128)) for c in range(3)])
                for i in range(8):
                    cs=slice(128*i,128*i+128)
                    T=st[0:8,cs]; I=[st[8+8*c:16+8*c,cs] for c in range(3)]
                    for m,rs in enumerate(rows):
                        aa=jnp.exp2(src_[8*(jg+m):8*(jg+m)+8,cs])
                        w=T*aa; T=T-w
                        for c in range(3): I[c]=I[c]+w*cols[m][c]
                        al[rs,cs]=aa; ws[rs,cs]=w
                    st[0:8,cs]=T
                    for c in range(3): st[8+8*c:16+8*c,cs]=I[c]
        st[0:8,:]=jnp.ones((8,PIX),f32)
        st[8:32,:]=jnp.zeros((24,PIX),f32)
        mm(0,0,eA)
        def fwd(b,_):
            nb=jnp.minimum(b+1,cnt-1)
            @pl.when(b%2==0)
            def _():
                mm(nb,0,eB); fblock(b,eA)
            @pl.when(b%2==1)
            def _():
                mm(nb,0,eA); fblock(b,eB)
            return 0
        lax.fori_loop(0,cnt,fwd,0)
        K=st[0:8,:]
        Cc=sum(st[8+8*c:16+8*c,:]*cots[8*c:8*c+8,:] for c in range(3))
        P=[jnp.ones((1,PIX),f32)]
        for s in range(7): P.append(P[-1]*K[s:s+1])
        V=[jnp.zeros((1,PIX),f32)]
        for s in range(7,0,-1): V.append(Cc[s:s+1]+K[s:s+1]*V[-1])
        Pv=jnp.concatenate(P,axis=0); V0=jnp.concatenate(V[::-1],axis=0)
        pref[...]=Pv
        lane128=lax.broadcasted_iota(jnp.int32,(8,128),1)//8
        def sums(sb_,zb_,r0):
            ra=jnp.dot(sb_[0:256],wa[...],preferred_element_type=f32)
            rc=jnp.dot(sb_[256:384],wb[...],preferred_element_type=f32)
            res[pl.ds(pl.multiple_of(r0,8),128),:]=ra[0:128]+ra[128:]+rc+zb_[...]
        def block(r0,qb,sb_,zb_):
            for jg in range(16-BJ,-1,-BJ):
                S=[[None]*3 for _ in range(BJ)]; Z=[[None]*3 for _ in range(BJ)]
                for i in range(7,-1,-1):
                    cs=slice(128*i,128*i+128)
                    V=vref[:,cs]; Pm=pref[:,cs]; ct=[cots[8*c:8*c+8,cs] for c in range(3)]
                    for m in range(BJ-1,-1,-1):
                        rs=pl.ds(pl.multiple_of(r0+8*(jg+m),8),8)
                        d=qb[8*(jg+m):8*(jg+m)+8,cs]-V
                        w=ws[rs,cs]*Pm
                        e=w*d
                        V=V+al[rs,cs]*d
                        for c in range(3):
                            zc=w*ct[c]
                            Z[m][c]=zc if i==7 else Z[m][c]+zc
                        s=S[m]
                        if i==7: s[0]=e; s[1]=e; s[2]=e
                        else:
                            s[0]=s[0]+e
                            if i>=1: s[1]=s[1]+s[0]; s[2]=s[2]+s[1]
                    vref[:,cs]=V
                for m in range(BJ):
                    zz=jnp.zeros((8,128),f32)
                    for c in range(3):
                        zz=jnp.where(lane128==6+c,jnp.sum(Z[m][c],axis=1,keepdims=True),zz)
                    zb_[8*(jg+m):8*(jg+m)+8,:]=zz
                for jp in range(0,BJ,2):
                    j=8*(jg+jp)
                    for m in range(3):
                        x=jnp.concatenate([S[jp][m],S[jp+1][m]],axis=0)
                        xh=x.astype(bf16); xl=(x-xh.astype(f32)).astype(bf16)
                        if m<2:
                            sb_[j:j+16,128*m:128*m+128]=xh
                            sb_[128+j:128+j+16,128*m:128*m+128]=xl
                        else:
                            sb_[256+j:256+j+16,0:128]=xh
                            sb_[256+j:256+j+16,128:256]=xl
        vref[...]=V0
        mm(cnt-1,1,eA)
        def bwd(i,_):
            b=cnt-1-i
            r0=pl.multiple_of(b*128,128)
            nb=jnp.maximum(b-1,0)
            @pl.when(i%2==0)
            def _():
                mm(nb,1,eB)
                sums(sbB,zbB,r0+128)
                block(r0,eA,sbA,zbA)
            @pl.when(i%2==1)
            def _():
                mm(nb,1,eA)
                sums(sbA,zbA,r0+128)
                block(r0,eB,sbB,zbB)
            return 0
        lax.fori_loop(0,cnt,bwd,0)
        @pl.when(cnt%2==1)
        def _(): sums(sbA,zbA,0)
        @pl.when(cnt%2==0)
        def _(): sums(sbB,zbB,0)
        sub=lax.broadcasted_iota(jnp.int32,(16,128),1)%8
        def slote(tg,row0):
            M=[None]*8
            for t in range(8):
                for k in range(8):
                    x=res[pl.ds(jnp.minimum(row0,last-1),16,stride=8),:]
                    M[k]=x if t==0 else jnp.where(sub==t,x,M[k])
                    row0=step_row(row0)
            Mt=jnp.concatenate(M,axis=0).T
            row=lambda k: Mt[8*k:8*k+8,:]
            mxx,mxy,myy,mx,my,m1=[row(k) for k in range(6)]
            tr=pl.ds(pl.multiple_of(8*tg,8),8)
            u=fs[0,tr,:]-cx; v=fs[1,tr,:]-cy; A=fs[2,tr,:]; B=fs[3,tr,:]; C=fs[4,tr,:]
            sx=mx-u*m1; sy=my-v*m1
            sxx=mxx-2.0*u*mx+u*u*m1
            syy=myy-2.0*v*my+v*v*m1
            sxy=mxy-u*my-v*mx+u*v*m1
            o=[A*sx+B*sy,B*sx+C*sy,-0.5*sxx,-sxy,-0.5*syy,m1]+[row(6+c) for c in range(3)]
            for t in range(8):
                @pl.when(8*tg+t<cnt)
                def _(t=t):
                    ow=ints_ref[2*who,0,ti*32+8*tg+t]//16
                    for f in range(9): out_ref[ow,f]=o[f][t:t+1,:]
            return row0
        lax.fori_loop(0,(cnt+7)//8,slote,0)
        return 0
    lax.fori_loop(0,8,tile,0)
def tiles(ints,feat,cot):
    sm=pl.BlockSpec(memory_space=pltpu.SMEM); vm=pl.BlockSpec(memory_space=pltpu.VMEM)
    return pl.pallas_call(tiles_kernel,out_shape=jax.ShapeDtypeStruct((2,128,9,1,128),f32),
        in_specs=[sm,vm,vm],out_specs=vm,
        scratch_shapes=[pltpu.VMEM((9,32,128),f32),pltpu.VMEM((32,16,128),f32),pltpu.VMEM((4096+128,128),f32),
            pltpu.VMEM((48,2*PIX),f32),pltpu.VMEM((256,128),bf16),pltpu.VMEM((256,128),bf16),pltpu.VMEM((8,PIX),f32),pltpu.VMEM((8,PIX),f32),
            pltpu.VMEM((32,PIX),f32),pltpu.VMEM((24,PIX),f32),pltpu.VMEM((48,2*PIX),bf16)]
            +[pltpu.VMEM((4096,PIX),f32)]*2+[pltpu.VMEM((128,PIX),f32)]*2
            +[pltpu.VMEM((384,256),bf16),pltpu.VMEM((128,128),f32)]*2+[pltpu.VMEM((4096+128,128),f32)],
        compiler_params=pltpu.CompilerParams(vmem_limit_bytes=67043328))(ints,feat,cot)


def load_params(p_ref):
    return [p_ref[row : row + 1, :].reshape(16, BLOCK) for row in range(59)]


def screen_rows(rows):
    return screen(rows, 1024.0, 512.0, 256.0)


LAG = 16


def everyone(me, n, act):
    def step(k, _):
        act(lax.rem(me + k, n))
        return 0

    lax.fori_loop(1, n, step, 0)


def lagged(me, n, fill, ship):
    def first(k, _):
        fill(lax.rem(me + k, n))
        return 0

    def both(k, _):
        fill(lax.rem(me + k, n))
        ship(lax.rem(me + k - LAG, n))
        return 0

    def last(k, _):
        ship(lax.rem(me + k, n))
        return 0

    lax.fori_loop(0, LAG + 1, first, 0)
    lax.fori_loop(LAG + 1, n, both, 0)
    lax.fori_loop(n - LAG, n, last, 0)


def send(src, dst, ssem, rsem, peer):
    return pltpu.make_async_remote_copy(
        src_ref=src,
        dst_ref=dst,
        send_sem=ssem,
        recv_sem=rsem,
        device_id=(peer,),
        device_id_type=pl.DeviceIdType.MESH,
    )


def all_but_one(ref, sem):
    rest = ref.at[pl.ds(0, ref.shape[0] - 1)]
    return pltpu.make_async_copy(rest, rest, sem)


def greet(me, n):
    bar = pltpu.get_barrier_semaphore()
    everyone(
        me,
        n,
        lambda peer: pl.semaphore_signal(bar, inc=1, device_id=(peer,), device_id_type=pl.DeviceIdType.MESH),
    )
    return bar


def forward_kernel(
    blk_ref, cnt_ref, p_ref, cot_ref, pair_ref, feat_ref, cot2_ref, idx_ref, ints_ref, lists, fsc, outbox, idxs, sems
):
    n = lax.axis_size("dev")
    me = lax.axis_index("dev")
    partner = me + 1 - 2 * lax.rem(me, 2)
    bar = greet(me, n)
    lane = lax.broadcasted_iota(jnp.int32, (1, 128), 1)
    ints_ref[0] = jnp.concatenate([blk_ref[k : k + 1, :] for k in range(4)], axis=1)
    ints_ref[1] = sum(jnp.where(lane == k, cnt_ref[k], 0) for k in range(4))
    for f, value in enumerate(screen_rows(load_params(p_ref))):
        fsc[f] = jnp.maximum(value, -1000.0) if f == 5 else value
    own_list = pltpu.make_async_copy(ints_ref.at[0], lists.at[me], sems.at[0])
    own_ints = pltpu.make_async_copy(ints_ref, pair_ref.at[pl.ds(0, 2)], sems.at[1])
    own_cot = pltpu.make_async_copy(cot_ref, cot2_ref.at[0], sems.at[2])
    own_list.start()
    own_ints.start()
    own_cot.start()
    pl.semaphore_wait(bar, n - 1)
    everyone(me, n, lambda peer: send(ints_ref.at[0], lists.at[me], sems.at[3], sems.at[4], peer).start())
    pair_ints = send(ints_ref, pair_ref.at[pl.ds(2, 2)], sems.at[5], sems.at[6], partner)
    pair_cot = send(cot_ref, cot2_ref.at[1], sems.at[7], sems.at[8], partner)
    pair_ints.start()
    pair_cot.start()
    own_list.wait()
    all_but_one(lists, sems.at[4]).wait()
    flat = lists[...].reshape(128, 128)
    asked = jnp.sum(jnp.where(flat >> 4 == me, flat & 15, 0).astype(f32), axis=1, keepdims=True)
    idx_ref[...] = jnp.broadcast_to(asked, (128, 128)).T[0:1].astype(jnp.int32)
    to_scalar = pltpu.make_async_copy(idx_ref, idxs, sems.at[9])
    to_scalar.start()
    to_scalar.wait()

    def put(d):
        for f in range(9):
            outbox[d, f] = fsc[f, pl.ds(idxs[0, d] & 15, 1), :]

    lagged(me, n, put, lambda peer: send(outbox.at[peer], feat_ref.at[0, me], sems.at[11], sems.at[12], peer).start())
    own_feat = pltpu.make_async_copy(outbox.at[me], feat_ref.at[0, me], sems.at[10])
    own_feat.start()
    all_but_one(lists, sems.at[3]).wait()
    own_ints.wait()
    own_cot.wait()
    own_feat.wait()
    pair_ints.wait()
    pair_cot.wait()
    all_but_one(outbox, sems.at[12]).wait()
    pair_feat = send(feat_ref.at[0], feat_ref.at[1], sems.at[13], sems.at[14], partner)
    pair_feat.start()
    all_but_one(outbox, sems.at[11]).wait()
    pair_feat.wait()


def back_kernel(grad_ref, recv_ref, theirs, outbox, sems):
    n = lax.axis_size("dev")
    me = lax.axis_index("dev")
    partner = me + 1 - 2 * lax.rem(me, 2)
    bar = greet(me, n)
    pl.semaphore_wait(bar, n - 1)
    pair = send(grad_ref.at[1], theirs, sems.at[0], sems.at[1], partner)
    pair.start()
    pair.wait_recv()

    def add(d):
        for f in range(9):
            outbox[d, f] = grad_ref[0, d, f] + theirs[d, f]

    lagged(me, n, add, lambda peer: send(outbox.at[peer], recv_ref.at[me], sems.at[3], sems.at[4], peer).start())
    own = pltpu.make_async_copy(outbox.at[me], recv_ref.at[me], sems.at[2])
    own.start()
    pair.wait_send()
    own.wait()
    all_but_one(outbox, sems.at[3]).wait()
    all_but_one(recv_ref, sems.at[4]).wait()


def final_kernel(idx_ref, p_ref, recv_ref, out_ref):
    rows = lax.broadcasted_iota(jnp.int32, (16, BLOCK), 0)

    def add(d, acc):
        hit = rows == idx_ref[0, d]
        return tuple(
            acc[f] + jnp.where(hit, jnp.broadcast_to(recv_ref[d, f], (16, BLOCK)), 0.0) for f in range(9)
        )

    zeros = tuple(jnp.zeros((16, BLOCK), f32) for _ in range(9))
    grads = list(lax.fori_loop(0, 128, add, zeros, unroll=4))
    pullback = jax.vjp(screen_rows, load_params(p_ref))[1]
    grads[5] = grads[5] * (1.0 / LOG2E)
    for row, value in enumerate(pullback(grads)[0]):
        out_ref[row : row + 1, :] = value.reshape(1, 2048)


def body(params, blocks, counts, pixel_grad):
    sm = pl.BlockSpec(memory_space=pltpu.SMEM)
    vm = pl.BlockSpec(memory_space=pltpu.VMEM)
    block_sums = jax.ShapeDtypeStruct((128, 9, 1, 128), f32)
    pair, feat, cot, idx = pl.pallas_call(
        forward_kernel,
        out_shape=[
            jax.ShapeDtypeStruct((4, 1, 128), jnp.int32),
            jax.ShapeDtypeStruct((2, 128, 9, 1, 128), f32),
            jax.ShapeDtypeStruct((2, 3, 4096), f32),
            jax.ShapeDtypeStruct((1, 128), jnp.int32),
        ],
        in_specs=[vm, sm, vm, vm],
        out_specs=[vm, vm, vm, vm],
        scratch_shapes=[
            pltpu.VMEM((2, 1, 128), jnp.int32),
            pltpu.VMEM((128, 1, 128), jnp.int32),
            pltpu.VMEM((9, 16, 128), f32),
            pltpu.VMEM((128, 9, 1, 128), f32),
            pltpu.SMEM((1, 128), jnp.int32),
            pltpu.SemaphoreType.DMA((15,)),
        ],
        compiler_params=pltpu.CompilerParams(collective_id=0, has_side_effects=True),
    )(blocks, counts, params, pixel_grad)
    grads = tiles(pair, feat, cot)
    back = pl.pallas_call(
        back_kernel,
        out_shape=block_sums,
        in_specs=[vm],
        out_specs=vm,
        scratch_shapes=[
            pltpu.VMEM((128, 9, 1, 128), f32),
            pltpu.VMEM((128, 9, 1, 128), f32),
            pltpu.SemaphoreType.DMA((5,)),
        ],
        compiler_params=pltpu.CompilerParams(collective_id=1, has_side_effects=True),
    )(grads)
    return pl.pallas_call(
        final_kernel,
        out_shape=jax.ShapeDtypeStruct((59, 2048), f32),
        in_specs=[sm, vm, vm],
        out_specs=vm,
    )(idx, params, back)


def solution(mesh):
    return jax.shard_map(
        body,
        mesh=mesh,
        in_specs=(P(None, "dev"), P("dev", None), P("dev"), P(None, "dev")),
        out_specs=P(None, "dev"),
        check_vma=False,
    )
```

```python
import jax
import jax.numpy as jnp
from jax import lax
from jax.experimental import pallas as pl
from jax.experimental.pallas import tpu as pltpu
from jax.sharding import PartitionSpec as P

LOG2E = 1.4426950408889634
sh_zero = 0.28209479177387814
sh_one = 0.4886025119029199
sh_two = [
    1.0925484305920792,
    -1.0925484305920792,
    0.31539156525252005,
    -1.0925484305920792,
    0.5462742152960396,
]
sh_three = [
    -0.5900435899266435,
    2.890611442640554,
    -0.4570457994644658,
    0.3731763325901154,
    -0.4570457994644658,
    1.445305721320277,
    -0.5900435899266435,
]


def sh_basis(dir_x, dir_y, dir_z):
    sq_x = dir_x * dir_x
    sq_y = dir_y * dir_y
    sq_z = dir_z * dir_z
    return [
        sh_zero + 0.0 * dir_x,
        -sh_one * dir_y,
        sh_one * dir_z,
        -sh_one * dir_x,
        sh_two[0] * dir_x * dir_y,
        sh_two[1] * dir_y * dir_z,
        sh_two[2] * (2.0 * sq_z - sq_x - sq_y),
        sh_two[3] * dir_x * dir_z,
        sh_two[4] * (sq_x - sq_y),
        sh_three[0] * dir_y * (3.0 * sq_x - sq_y),
        sh_three[1] * dir_x * dir_y * dir_z,
        sh_three[2] * dir_y * (4.0 * sq_z - sq_x - sq_y),
        sh_three[3] * dir_z * (2.0 * sq_z - 3.0 * sq_x - 3.0 * sq_y),
        sh_three[4] * dir_x * (4.0 * sq_z - sq_x - sq_y),
        sh_three[5] * dir_z * (sq_x - sq_y),
        sh_three[6] * dir_x * (sq_x - 3.0 * sq_y),
    ]


def screen(params, focal_len, centre_x, centre_y):
    mean_x, mean_y, depths = (params[0], params[1], params[2])
    scales = [jnp.exp(params[row]) for row in range(3, 6)]
    quat = params[6:10]
    norm = jnp.sqrt(quat[0] * quat[0] + quat[1] * quat[1] + quat[2] * quat[2] + quat[3] * quat[3])
    quat = [part / norm for part in quat]
    quat_r, quat_i, quat_j, quat_k = (quat[0], quat[1], quat[2], quat[3])
    rotation = [
        [
            1.0 - 2.0 * (quat_j * quat_j + quat_k * quat_k),
            2.0 * (quat_i * quat_j - quat_r * quat_k),
            2.0 * (quat_i * quat_k + quat_r * quat_j),
        ],
        [
            2.0 * (quat_i * quat_j + quat_r * quat_k),
            1.0 - 2.0 * (quat_i * quat_i + quat_k * quat_k),
            2.0 * (quat_j * quat_k - quat_r * quat_i),
        ],
        [
            2.0 * (quat_i * quat_k - quat_r * quat_j),
            2.0 * (quat_j * quat_k + quat_r * quat_i),
            1.0 - 2.0 * (quat_i * quat_i + quat_j * quat_j),
        ],
    ]
    inv_z = 1.0 / depths
    diag_jac = focal_len * inv_z
    side_x = -focal_len * mean_x * inv_z * inv_z
    side_y = -focal_len * mean_y * inv_z * inv_z
    upper = [
        (diag_jac * rotation[0][column] + side_x * rotation[2][column]) * scales[column]
        for column in range(3)
    ]
    lower = [
        (diag_jac * rotation[1][column] + side_y * rotation[2][column]) * scales[column]
        for column in range(3)
    ]
    cov_xx = upper[0] * upper[0] + upper[1] * upper[1] + upper[2] * upper[2] + 0.3
    cov_xy = upper[0] * lower[0] + upper[1] * lower[1] + upper[2] * lower[2]
    cov_yy = lower[0] * lower[0] + lower[1] * lower[1] + lower[2] * lower[2] + 0.3
    determ = cov_xx * cov_yy - cov_xy * cov_xy
    screen_u = focal_len * mean_x * inv_z + centre_x
    screen_v = focal_len * mean_y * inv_z + centre_y
    logit = params[10]
    log_opacity = (logit - jnp.log1p(jnp.exp(logit))) * LOG2E
    distance = jnp.sqrt(mean_x * mean_x + mean_y * mean_y + depths * depths)
    basis = sh_basis(mean_x / distance, mean_y / distance, depths / distance)
    colors = [
        0.5
        + sum((basis[harmonic] * params[11 + 16 * channel + harmonic] for harmonic in range(16)))
        for channel in range(3)
    ]
    return [screen_u, screen_v, cov_yy / determ, -cov_xy / determ, cov_xx / determ, log_opacity] + colors
BLOCK=128; SIDE=32; TX=32; PIX=1024; MAXB=32
BU=4; FJ=1; BJ=2
f32=jnp.float32; bf16=jnp.bfloat16

def split3(x):
    hi=x.astype(bf16).astype(f32); r=x-hi
    mid=r.astype(bf16).astype(f32); lo=r-mid
    return hi,mid,lo

def tiles_kernel(ints_ref, feat2_ref, cot2_ref, out2_ref,
                 fs, xs, lhs, rhs, wa, wb, pref, vref, st, cots, rbs, al, ws, eA, eB, sbA, zbA, sbB, zbB, res):
    me=lax.axis_index("dev")
    odd=me%2
    mine=[ints_ref[1,0,k] for k in range(4)]; other=[ints_ref[3,0,k] for k in range(4)]
    sm_,so_=sum(mine),sum(other)
    own_full=jnp.logical_or(sm_>so_,jnp.logical_and(sm_==so_,odd==0))
    full=[jnp.where(own_full,a,b) for a,b in zip(mine,other)]
    hi_=jnp.maximum(sm_,so_); lo_=jnp.minimum(sm_,so_)
    best,pick=hi_,jnp.int32(0)
    for sub in range(1,15):
        moved=sum(full[k] for k in range(4) if sub>>k&1)
        top=jnp.maximum(hi_-moved,lo_+moved)
        better=top<best
        pick=jnp.where(better,sub,pick); best=jnp.where(better,top,best)
    lane=lax.broadcasted_iota(jnp.int32,(1,PIX),1)
    X=(lane%SIDE-16).astype(f32); Y=(lane//SIDE-16).astype(f32)
    mono=[X*X,X*Y,Y*Y,X,Y,jnp.ones_like(X)]
    out2_ref[...]=jnp.zeros_like(out2_ref)
    rhs[...]=jnp.zeros_like(rhs)
    for part in range(3):
        for k in range(6): rhs[16*part+k:16*part+k+1,0:PIX]=mono[k]
    x1=X[:,0:128]; y1=(lax.broadcasted_iota(jnp.int32,(1,128),1)//SIDE-16).astype(f32); o1=jnp.ones_like(x1); z1=jnp.zeros_like(x1)
    pad=jnp.zeros((80,128),f32)
    rep=lambda rows: jnp.concatenate([jnp.broadcast_to(x,(8,128)) for x in rows]+[pad],axis=0).T
    W0=rep([x1*x1,x1*y1,y1*y1,x1,y1,o1])
    W1=rep([z1,4.0*x1,8.0*y1-16.0,z1,4.0*o1,z1])
    W2=rep([z1,z1,32.0*o1,z1,z1,z1])
    wa[...]=jnp.concatenate([W0,W1],axis=0).astype(bf16)
    wb[...]=jnp.concatenate([W2,W2],axis=0).astype(bf16)
    def tile(tx,_):
        who=tx//4; ti=tx%4
        gone=jnp.bitwise_and(jnp.right_shift(pick,ti),1)
        here=jnp.where(own_full,jnp.logical_and(who==0,gone==0),jnp.logical_or(who==0,gone==1))
        @pl.when(here)
        def _():
            one_tile(who,ti)
        return 0
    def one_tile(who,ti):
        feat_ref=feat2_ref.at[who]; cot_ref=cot2_ref.at[who]; out_ref=out2_ref.at[who]
        cnt=ints_ref[2*who+1,0,ti]
        tid=jnp.where(who==0,me,me+1-2*odd)*4+ti
        cx=((tid%TX)*SIDE).astype(f32)+16.5
        cy=((tid//TX)*SIDE).astype(f32)+16.5
        last=128*cnt
        def step_row(r):
            r=r+128
            return jnp.where(r>=last,r-last+1,r)
        def gat(tg,_):
            for t in range(4):
                ow=jnp.right_shift(ints_ref[2*who,0,ti*32+4*tg+t],4)
                for f in range(9): fs[f,pl.ds(4*tg+t,1),:]=feat_ref[ow,f]
            return 0
        lax.fori_loop(0,(cnt+3)//4,gat,0)
        u=fs[0]-cx; v=fs[1]-cy; A=fs[2]; B=fs[3]; C=fs[4]; lo2=fs[5]
        p=A*u+B*v; r=B*u+C*v
        cf=[(-0.5*LOG2E)*A,(-LOG2E)*B,(-0.5*LOG2E)*C,LOG2E*p,LOG2E*r,(-0.5*LOG2E)*(u*p+v*r)+lo2,
            fs[6],fs[7],fs[8],fs[6],fs[7],fs[8],fs[6],fs[7],fs[8]]
        for k in range(15): xs[:,k,:]=cf[k]
        xs[:,15,:]=jnp.zeros_like(u)
        for c in range(3):
            ct=cot_ref[c:c+1,pl.ds(pl.multiple_of(ti*PIX,PIX),PIX)]
            h,m,l=split3(ct)
            for part in range(3):
                b=16*part+6+c
                rhs[b:b+1,PIX:]=h; rhs[b+3:b+4,PIX:]=m; rhs[b+6:b+7,PIX:]=l
        for c in range(3):
            cots[8*c:8*c+8,:]=jnp.broadcast_to(cot_ref[c:c+1,pl.ds(pl.multiple_of(ti*PIX,PIX),PIX)],(8,PIX))
        def slotp(tg,row0):
            for i in range(BU):
                x=xs[BU*tg+i]
                h,m,l=split3(x)
                y=jnp.concatenate([h,m,l,x,jnp.zeros((64,128),f32)],axis=0).T
                for k in range(8):
                    lhs[pl.ds(jnp.where(BU*tg+i<cnt,row0,4096),16,stride=8),:]=y[16*k:16*k+16,:]
                    row0=step_row(row0)
            return row0
        lax.fori_loop(0,(cnt+BU-1)//BU,slotp,0)
        rbs[...]=rhs[...].astype(bf16)
        def mm(b,h,dst):
            L=lhs[pl.ds(pl.multiple_of(b*128,128),128),0:48].astype(bf16)
            dst[...]=jnp.dot(L,rbs[:,h*PIX:h*PIX+PIX],preferred_element_type=f32)
        def fblock(b,src_):
            for jg in range(0,16,FJ):
                rows=[pl.ds(pl.multiple_of(b*128+8*jj,8),8) for jj in range(jg,jg+FJ)]
                cols=[]
                for rs in rows:
                    lrow=lhs[rs,:]
                    cols.append([jnp.broadcast_to(lrow[:,54+c:55+c],(8,128)) for c in range(3)])
                for i in range(8):
                    cs=slice(128*i,128*i+128)
                    T=st[0:8,cs]; I=[st[8+8*c:16+8*c,cs] for c in range(3)]
                    for m,rs in enumerate(rows):
                        aa=jnp.exp2(src_[8*(jg+m):8*(jg+m)+8,cs])
                        w=T*aa; T=T-w
                        for c in range(3): I[c]=I[c]+w*cols[m][c]
                        al[rs,cs]=aa; ws[rs,cs]=w
                    st[0:8,cs]=T
                    for c in range(3): st[8+8*c:16+8*c,cs]=I[c]
        st[0:8,:]=jnp.ones((8,PIX),f32)
        st[8:32,:]=jnp.zeros((24,PIX),f32)
        mm(0,0,eA)
        def fwd(b,_):
            nb=jnp.minimum(b+1,cnt-1)
            @pl.when(b%2==0)
            def _():
                mm(nb,0,eB); fblock(b,eA)
            @pl.when(b%2==1)
            def _():
                mm(nb,0,eA); fblock(b,eB)
            return 0
        lax.fori_loop(0,cnt,fwd,0)
        K=st[0:8,:]
        Cc=sum(st[8+8*c:16+8*c,:]*cots[8*c:8*c+8,:] for c in range(3))
        P=[jnp.ones((1,PIX),f32)]
        for s in range(7): P.append(P[-1]*K[s:s+1])
        V=[jnp.zeros((1,PIX),f32)]
        for s in range(7,0,-1): V.append(Cc[s:s+1]+K[s:s+1]*V[-1])
        Pv=jnp.concatenate(P,axis=0); V0=jnp.concatenate(V[::-1],axis=0)
        pref[...]=Pv
        lane128=lax.broadcasted_iota(jnp.int32,(8,128),1)//8
        def sums(sb_,zb_,r0):
            ra=jnp.dot(sb_[0:256],wa[...],preferred_element_type=f32)
            rc=jnp.dot(sb_[256:384],wb[...],preferred_element_type=f32)
            res[pl.ds(pl.multiple_of(r0,8),128),:]=ra[0:128]+ra[128:]+rc+zb_[...]
        def block(r0,qb,sb_,zb_):
            for jg in range(16-BJ,-1,-BJ):
                S=[[None]*3 for _ in range(BJ)]; Z=[[None]*3 for _ in range(BJ)]
                for i in range(7,-1,-1):
                    cs=slice(128*i,128*i+128)
                    V=vref[:,cs]; Pm=pref[:,cs]; ct=[cots[8*c:8*c+8,cs] for c in range(3)]
                    for m in range(BJ-1,-1,-1):
                        rs=pl.ds(pl.multiple_of(r0+8*(jg+m),8),8)
                        d=qb[8*(jg+m):8*(jg+m)+8,cs]-V
                        w=ws[rs,cs]*Pm
                        e=w*d
                        V=V+al[rs,cs]*d
                        for c in range(3):
                            zc=w*ct[c]
                            Z[m][c]=zc if i==7 else Z[m][c]+zc
                        s=S[m]
                        if i==7: s[0]=e; s[1]=e; s[2]=e
                        else:
                            s[0]=s[0]+e
                            if i>=1: s[1]=s[1]+s[0]; s[2]=s[2]+s[1]
                    vref[:,cs]=V
                for m in range(BJ):
                    zz=jnp.zeros((8,128),f32)
                    for c in range(3):
                        zz=jnp.where(lane128==6+c,jnp.sum(Z[m][c],axis=1,keepdims=True),zz)
                    zb_[8*(jg+m):8*(jg+m)+8,:]=zz
                for jp in range(0,BJ,2):
                    j=8*(jg+jp)
                    for m in range(3):
                        x=jnp.concatenate([S[jp][m],S[jp+1][m]],axis=0)
                        xh=x.astype(bf16); xl=(x-xh.astype(f32)).astype(bf16)
                        if m<2:
                            sb_[j:j+16,128*m:128*m+128]=xh
                            sb_[128+j:128+j+16,128*m:128*m+128]=xl
                        else:
                            sb_[256+j:256+j+16,0:128]=xh
                            sb_[256+j:256+j+16,128:256]=xl
        vref[...]=V0
        mm(cnt-1,1,eA)
        def bwd(i,_):
            b=cnt-1-i
            r0=pl.multiple_of(b*128,128)
            nb=jnp.maximum(b-1,0)
            @pl.when(i%2==0)
            def _():
                mm(nb,1,eB)
                sums(sbB,zbB,r0+128)
                block(r0,eA,sbA,zbA)
            @pl.when(i%2==1)
            def _():
                mm(nb,1,eA)
                sums(sbA,zbA,r0+128)
                block(r0,eB,sbB,zbB)
            return 0
        lax.fori_loop(0,cnt,bwd,0)
        @pl.when(cnt%2==1)
        def _(): sums(sbA,zbA,0)
        @pl.when(cnt%2==0)
        def _(): sums(sbB,zbB,0)
        sub=lax.broadcasted_iota(jnp.int32,(16,128),1)%8
        def slote(tg,row0):
            M=[None]*8
            for t in range(8):
                for k in range(8):
                    x=res[pl.ds(jnp.minimum(row0,last-1),16,stride=8),:]
                    M[k]=x if t==0 else jnp.where(sub==t,x,M[k])
                    row0=step_row(row0)
            Mt=jnp.concatenate(M,axis=0).T
            row=lambda k: Mt[8*k:8*k+8,:]
            mxx,mxy,myy,mx,my,m1=[row(k) for k in range(6)]
            tr=pl.ds(pl.multiple_of(8*tg,8),8)
            u=fs[0,tr,:]-cx; v=fs[1,tr,:]-cy; A=fs[2,tr,:]; B=fs[3,tr,:]; C=fs[4,tr,:]
            sx=mx-u*m1; sy=my-v*m1
            sxx=mxx-2.0*u*mx+u*u*m1
            syy=myy-2.0*v*my+v*v*m1
            sxy=mxy-u*my-v*mx+u*v*m1
            o=[A*sx+B*sy,B*sx+C*sy,-0.5*sxx,-sxy,-0.5*syy,m1]+[row(6+c) for c in range(3)]
            live=lax.broadcasted_iota(jnp.int32,(8,128),0)<cnt-8*tg
            o=[jnp.where(live,x,0.0) for x in o]
            for t in range(8):
                ow=jnp.right_shift(ints_ref[2*who,0,ti*32+8*tg+t],4)
                for f in range(9): out_ref[ow,f]=o[f][t:t+1,:]
            return row0
        lax.fori_loop(0,(cnt+7)//8,slote,0)
        return 0
    lax.fori_loop(0,8,tile,0)
def tiles(ints,feat,cot):
    sm=pl.BlockSpec(memory_space=pltpu.SMEM); vm=pl.BlockSpec(memory_space=pltpu.VMEM)
    return pl.pallas_call(tiles_kernel,out_shape=jax.ShapeDtypeStruct((2,128,9,1,128),f32),
        in_specs=[sm,vm,vm],out_specs=vm,
        scratch_shapes=[pltpu.VMEM((9,32,128),f32),pltpu.VMEM((32,16,128),f32),pltpu.VMEM((4096+128,128),f32),
            pltpu.VMEM((48,2*PIX),f32),pltpu.VMEM((256,128),bf16),pltpu.VMEM((256,128),bf16),pltpu.VMEM((8,PIX),f32),pltpu.VMEM((8,PIX),f32),
            pltpu.VMEM((32,PIX),f32),pltpu.VMEM((24,PIX),f32),pltpu.VMEM((48,2*PIX),bf16)]
            +[pltpu.VMEM((4096,PIX),f32)]*2+[pltpu.VMEM((128,PIX),f32)]*2
            +[pltpu.VMEM((384,256),bf16),pltpu.VMEM((128,128),f32)]*2+[pltpu.VMEM((4096+128,128),f32)],
        compiler_params=pltpu.CompilerParams(vmem_limit_bytes=67043328))(ints,feat,cot)


def load_params(p_ref):
    return [p_ref[row : row + 1, :].reshape(16, BLOCK) for row in range(59)]


def screen_rows(rows):
    return screen(rows, 1024.0, 512.0, 256.0)


LAG = 16


def everyone(me, n, act):
    def step(k, _):
        act(lax.rem(me + k, n))
        return 0

    lax.fori_loop(1, n, step, 0)


def lagged(me, n, fill, ship):
    def first(k, _):
        fill(lax.rem(me + k, n))
        return 0

    def both(k, _):
        fill(lax.rem(me + k, n))
        ship(lax.rem(me + k - LAG, n))
        return 0

    def last(k, _):
        ship(lax.rem(me + k, n))
        return 0

    lax.fori_loop(0, LAG + 1, first, 0)
    lax.fori_loop(LAG + 1, n, both, 0)
    lax.fori_loop(n - LAG, n, last, 0)


def send(src, dst, ssem, rsem, peer):
    return pltpu.make_async_remote_copy(
        src_ref=src,
        dst_ref=dst,
        send_sem=ssem,
        recv_sem=rsem,
        device_id=(peer,),
        device_id_type=pl.DeviceIdType.MESH,
    )


def all_but_one(ref, sem):
    rest = ref.at[pl.ds(0, ref.shape[0] - 1)]
    return pltpu.make_async_copy(rest, rest, sem)


def greet(me, n):
    bar = pltpu.get_barrier_semaphore()
    everyone(
        me,
        n,
        lambda peer: pl.semaphore_signal(bar, inc=1, device_id=(peer,), device_id_type=pl.DeviceIdType.MESH),
    )
    return bar


def forward_kernel(
    blk_ref, cnt_ref, p_ref, cot_ref, pair_ref, feat_ref, cot2_ref, idx_ref, ints_ref, lists, fsc, outbox, idxs, sems
):
    n = lax.axis_size("dev")
    me = lax.axis_index("dev")
    partner = me + 1 - 2 * lax.rem(me, 2)
    bar = greet(me, n)
    lane = lax.broadcasted_iota(jnp.int32, (1, 128), 1)
    ints_ref[0] = jnp.concatenate([blk_ref[k : k + 1, :] for k in range(4)], axis=1)
    ints_ref[1] = sum(jnp.where(lane == k, cnt_ref[k], 0) for k in range(4))
    for f, value in enumerate(screen_rows(load_params(p_ref))):
        fsc[f] = jnp.maximum(value, -1000.0) if f == 5 else value
    own_list = pltpu.make_async_copy(ints_ref.at[0], lists.at[me], sems.at[0])
    own_ints = pltpu.make_async_copy(ints_ref, pair_ref.at[pl.ds(0, 2)], sems.at[1])
    own_cot = pltpu.make_async_copy(cot_ref, cot2_ref.at[0], sems.at[2])
    own_list.start()
    own_ints.start()
    own_cot.start()
    pl.semaphore_wait(bar, n - 1)
    everyone(me, n, lambda peer: send(ints_ref.at[0], lists.at[me], sems.at[3], sems.at[4], peer).start())
    pair_ints = send(ints_ref, pair_ref.at[pl.ds(2, 2)], sems.at[5], sems.at[6], partner)
    pair_cot = send(cot_ref, cot2_ref.at[1], sems.at[7], sems.at[8], partner)
    pair_ints.start()
    pair_cot.start()
    own_list.wait()
    all_but_one(lists, sems.at[4]).wait()
    flat = lists[...].reshape(128, 128)
    asked = jnp.sum(jnp.where(flat >> 4 == me, flat & 15, 0).astype(f32), axis=1, keepdims=True)
    idx_ref[...] = jnp.broadcast_to(asked, (128, 128)).T[0:1].astype(jnp.int32)
    to_scalar = pltpu.make_async_copy(idx_ref, idxs, sems.at[9])
    to_scalar.start()
    to_scalar.wait()

    def put(d):
        for f in range(9):
            outbox[d, f] = fsc[f, pl.ds(idxs[0, d] & 15, 1), :]

    lagged(me, n, put, lambda peer: send(outbox.at[peer], feat_ref.at[0, me], sems.at[11], sems.at[12], peer).start())
    own_feat = pltpu.make_async_copy(outbox.at[me], feat_ref.at[0, me], sems.at[10])
    own_feat.start()
    all_but_one(lists, sems.at[3]).wait()
    own_ints.wait()
    own_cot.wait()
    own_feat.wait()
    pair_ints.wait()
    pair_cot.wait()
    all_but_one(outbox, sems.at[12]).wait()
    pair_feat = send(feat_ref.at[0], feat_ref.at[1], sems.at[13], sems.at[14], partner)
    pair_feat.start()
    all_but_one(outbox, sems.at[11]).wait()
    pair_feat.wait()


def back_kernel(grad_ref, recv_ref, theirs, outbox, sems):
    n = lax.axis_size("dev")
    me = lax.axis_index("dev")
    partner = me + 1 - 2 * lax.rem(me, 2)
    bar = greet(me, n)
    pl.semaphore_wait(bar, n - 1)
    pair = send(grad_ref.at[1], theirs, sems.at[0], sems.at[1], partner)
    pair.start()
    pair.wait_recv()

    def add(d):
        for f in range(9):
            outbox[d, f] = grad_ref[0, d, f] + theirs[d, f]

    lagged(me, n, add, lambda peer: send(outbox.at[peer], recv_ref.at[me], sems.at[3], sems.at[4], peer).start())
    own = pltpu.make_async_copy(outbox.at[me], recv_ref.at[me], sems.at[2])
    own.start()
    pair.wait_send()
    own.wait()
    all_but_one(outbox, sems.at[3]).wait()
    all_but_one(recv_ref, sems.at[4]).wait()


def final_kernel(idx_ref, p_ref, recv_ref, out_ref):
    rows = lax.broadcasted_iota(jnp.int32, (16, BLOCK), 0)

    def add(d, acc):
        hit = rows == idx_ref[0, d]
        return tuple(
            acc[f] + jnp.where(hit, jnp.broadcast_to(recv_ref[d, f], (16, BLOCK)), 0.0) for f in range(9)
        )

    zeros = tuple(jnp.zeros((16, BLOCK), f32) for _ in range(9))
    grads = list(lax.fori_loop(0, 128, add, zeros, unroll=4))
    pullback = jax.vjp(screen_rows, load_params(p_ref))[1]
    grads[5] = grads[5] * (1.0 / LOG2E)
    for row, value in enumerate(pullback(grads)[0]):
        out_ref[row : row + 1, :] = value.reshape(1, 2048)


def body(params, blocks, counts, pixel_grad):
    sm = pl.BlockSpec(memory_space=pltpu.SMEM)
    vm = pl.BlockSpec(memory_space=pltpu.VMEM)
    block_sums = jax.ShapeDtypeStruct((128, 9, 1, 128), f32)
    pair, feat, cot, idx = pl.pallas_call(
        forward_kernel,
        out_shape=[
            jax.ShapeDtypeStruct((4, 1, 128), jnp.int32),
            jax.ShapeDtypeStruct((2, 128, 9, 1, 128), f32),
            jax.ShapeDtypeStruct((2, 3, 4096), f32),
            jax.ShapeDtypeStruct((1, 128), jnp.int32),
        ],
        in_specs=[vm, sm, vm, vm],
        out_specs=[vm, vm, vm, vm],
        scratch_shapes=[
            pltpu.VMEM((2, 1, 128), jnp.int32),
            pltpu.VMEM((128, 1, 128), jnp.int32),
            pltpu.VMEM((9, 16, 128), f32),
            pltpu.VMEM((128, 9, 1, 128), f32),
            pltpu.SMEM((1, 128), jnp.int32),
            pltpu.SemaphoreType.DMA((15,)),
        ],
        compiler_params=pltpu.CompilerParams(collective_id=0, has_side_effects=True),
    )(blocks, counts, params, pixel_grad)
    grads = tiles(pair, feat, cot)
    back = pl.pallas_call(
        back_kernel,
        out_shape=block_sums,
        in_specs=[vm],
        out_specs=vm,
        scratch_shapes=[
            pltpu.VMEM((128, 9, 1, 128), f32),
            pltpu.VMEM((128, 9, 1, 128), f32),
            pltpu.SemaphoreType.DMA((5,)),
        ],
        compiler_params=pltpu.CompilerParams(collective_id=1, has_side_effects=True),
    )(grads)
    return pl.pallas_call(
        final_kernel,
        out_shape=jax.ShapeDtypeStruct((59, 2048), f32),
        in_specs=[sm, vm, vm],
        out_specs=vm,
    )(idx, params, back)


def solution(mesh):
    return jax.shard_map(
        body,
        mesh=mesh,
        in_specs=(P(None, "dev"), P("dev", None), P("dev"), P(None, "dev")),
        out_specs=P(None, "dev"),
        check_vma=False,
    )
```

```python
import jax
import jax.numpy as jnp
from jax import lax
from jax.experimental import pallas as pl
from jax.experimental.pallas import tpu as pltpu
from jax.sharding import PartitionSpec as P

LOG2E = 1.4426950408889634
sh_zero = 0.28209479177387814
sh_one = 0.4886025119029199
sh_two = [
    1.0925484305920792,
    -1.0925484305920792,
    0.31539156525252005,
    -1.0925484305920792,
    0.5462742152960396,
]
sh_three = [
    -0.5900435899266435,
    2.890611442640554,
    -0.4570457994644658,
    0.3731763325901154,
    -0.4570457994644658,
    1.445305721320277,
    -0.5900435899266435,
]


def sh_basis(dir_x, dir_y, dir_z):
    sq_x = dir_x * dir_x
    sq_y = dir_y * dir_y
    sq_z = dir_z * dir_z
    return [
        sh_zero + 0.0 * dir_x,
        -sh_one * dir_y,
        sh_one * dir_z,
        -sh_one * dir_x,
        sh_two[0] * dir_x * dir_y,
        sh_two[1] * dir_y * dir_z,
        sh_two[2] * (2.0 * sq_z - sq_x - sq_y),
        sh_two[3] * dir_x * dir_z,
        sh_two[4] * (sq_x - sq_y),
        sh_three[0] * dir_y * (3.0 * sq_x - sq_y),
        sh_three[1] * dir_x * dir_y * dir_z,
        sh_three[2] * dir_y * (4.0 * sq_z - sq_x - sq_y),
        sh_three[3] * dir_z * (2.0 * sq_z - 3.0 * sq_x - 3.0 * sq_y),
        sh_three[4] * dir_x * (4.0 * sq_z - sq_x - sq_y),
        sh_three[5] * dir_z * (sq_x - sq_y),
        sh_three[6] * dir_x * (sq_x - 3.0 * sq_y),
    ]


def screen(params, focal_len, centre_x, centre_y):
    mean_x, mean_y, depths = (params[0], params[1], params[2])
    scales = [jnp.exp(params[row]) for row in range(3, 6)]
    quat = params[6:10]
    norm = jnp.sqrt(quat[0] * quat[0] + quat[1] * quat[1] + quat[2] * quat[2] + quat[3] * quat[3])
    quat = [part / norm for part in quat]
    quat_r, quat_i, quat_j, quat_k = (quat[0], quat[1], quat[2], quat[3])
    rotation = [
        [
            1.0 - 2.0 * (quat_j * quat_j + quat_k * quat_k),
            2.0 * (quat_i * quat_j - quat_r * quat_k),
            2.0 * (quat_i * quat_k + quat_r * quat_j),
        ],
        [
            2.0 * (quat_i * quat_j + quat_r * quat_k),
            1.0 - 2.0 * (quat_i * quat_i + quat_k * quat_k),
            2.0 * (quat_j * quat_k - quat_r * quat_i),
        ],
        [
            2.0 * (quat_i * quat_k - quat_r * quat_j),
            2.0 * (quat_j * quat_k + quat_r * quat_i),
            1.0 - 2.0 * (quat_i * quat_i + quat_j * quat_j),
        ],
    ]
    inv_z = 1.0 / depths
    diag_jac = focal_len * inv_z
    side_x = -focal_len * mean_x * inv_z * inv_z
    side_y = -focal_len * mean_y * inv_z * inv_z
    upper = [
        (diag_jac * rotation[0][column] + side_x * rotation[2][column]) * scales[column]
        for column in range(3)
    ]
    lower = [
        (diag_jac * rotation[1][column] + side_y * rotation[2][column]) * scales[column]
        for column in range(3)
    ]
    cov_xx = upper[0] * upper[0] + upper[1] * upper[1] + upper[2] * upper[2] + 0.3
    cov_xy = upper[0] * lower[0] + upper[1] * lower[1] + upper[2] * lower[2]
    cov_yy = lower[0] * lower[0] + lower[1] * lower[1] + lower[2] * lower[2] + 0.3
    determ = cov_xx * cov_yy - cov_xy * cov_xy
    screen_u = focal_len * mean_x * inv_z + centre_x
    screen_v = focal_len * mean_y * inv_z + centre_y
    logit = params[10]
    log_opacity = (logit - jnp.log1p(jnp.exp(logit))) * LOG2E
    distance = jnp.sqrt(mean_x * mean_x + mean_y * mean_y + depths * depths)
    basis = sh_basis(mean_x / distance, mean_y / distance, depths / distance)
    colors = [
        0.5
        + sum((basis[harmonic] * params[11 + 16 * channel + harmonic] for harmonic in range(16)))
        for channel in range(3)
    ]
    return [screen_u, screen_v, cov_yy / determ, -cov_xy / determ, cov_xx / determ, log_opacity] + colors
BLOCK=128; SIDE=32; TX=32; PIX=1024; MAXB=32
BU=8; FJ=1; BJ=2
f32=jnp.float32; bf16=jnp.bfloat16

def split3(x):
    hi=x.astype(bf16).astype(f32); r=x-hi
    mid=r.astype(bf16).astype(f32); lo=r-mid
    return hi,mid,lo

def tiles_kernel(ints_ref, feat2_ref, cot2_ref, out2_ref,
                 fs, xs, lhs, rhs, wa, wb, pref, vref, st, cots, rbs, al, ws, eA, eB, sbA, zbA, sbB, zbB, res):
    me=lax.axis_index("dev")
    odd=me%2
    mine=[ints_ref[1,0,k] for k in range(4)]; other=[ints_ref[3,0,k] for k in range(4)]
    sm_,so_=sum(mine),sum(other)
    own_full=jnp.logical_or(sm_>so_,jnp.logical_and(sm_==so_,odd==0))
    full=[jnp.where(own_full,a,b) for a,b in zip(mine,other)]
    hi_=jnp.maximum(sm_,so_); lo_=jnp.minimum(sm_,so_)
    best,pick=hi_,jnp.int32(0)
    for sub in range(1,15):
        moved=sum(full[k] for k in range(4) if sub>>k&1)
        top=jnp.maximum(hi_-moved,lo_+moved)
        better=top<best
        pick=jnp.where(better,sub,pick); best=jnp.where(better,top,best)
    lane=lax.broadcasted_iota(jnp.int32,(1,PIX),1)
    X=(lane%SIDE-16).astype(f32); Y=(lane//SIDE-16).astype(f32)
    mono=[X*X,X*Y,Y*Y,X,Y,jnp.ones_like(X)]
    out2_ref[...]=jnp.zeros_like(out2_ref)
    rhs[...]=jnp.zeros_like(rhs)
    for part in range(3):
        for k in range(6): rhs[16*part+k:16*part+k+1,0:PIX]=mono[k]
    x1=X[:,0:128]; y1=(lax.broadcasted_iota(jnp.int32,(1,128),1)//SIDE-16).astype(f32); o1=jnp.ones_like(x1); z1=jnp.zeros_like(x1)
    pad=jnp.zeros((80,128),f32)
    rep=lambda rows: jnp.concatenate([jnp.broadcast_to(x,(8,128)) for x in rows]+[pad],axis=0).T
    W0=rep([x1*x1,x1*y1,y1*y1,x1,y1,o1])
    W1=rep([z1,4.0*x1,8.0*y1-16.0,z1,4.0*o1,z1])
    W2=rep([z1,z1,32.0*o1,z1,z1,z1])
    wa[...]=jnp.concatenate([W0,W1],axis=0).astype(bf16)
    wb[...]=jnp.concatenate([W2,W2],axis=0).astype(bf16)
    def tile(tx,_):
        who=tx//4; ti=tx%4
        gone=jnp.bitwise_and(jnp.right_shift(pick,ti),1)
        here=jnp.where(own_full,jnp.logical_and(who==0,gone==0),jnp.logical_or(who==0,gone==1))
        @pl.when(here)
        def _():
            one_tile(who,ti)
        return 0
    def one_tile(who,ti):
        feat_ref=feat2_ref.at[who]; cot_ref=cot2_ref.at[who]; out_ref=out2_ref.at[who]
        cnt=ints_ref[2*who+1,0,ti]
        tid=jnp.where(who==0,me,me+1-2*odd)*4+ti
        cx=((tid%TX)*SIDE).astype(f32)+16.5
        cy=((tid//TX)*SIDE).astype(f32)+16.5
        last=128*cnt
        def step_row(r):
            r=r+128
            return jnp.where(r>=last,r-last+1,r)
        def gat(tg,_):
            for t in range(4):
                ow=jnp.right_shift(ints_ref[2*who,0,ti*32+4*tg+t],4)
                for f in range(9): fs[f,pl.ds(4*tg+t,1),:]=feat_ref[ow,f]
            return 0
        lax.fori_loop(0,(cnt+3)//4,gat,0)
        u=fs[0]-cx; v=fs[1]-cy; A=fs[2]; B=fs[3]; C=fs[4]; lo2=fs[5]
        p=A*u+B*v; r=B*u+C*v
        cf=[(-0.5*LOG2E)*A,(-LOG2E)*B,(-0.5*LOG2E)*C,LOG2E*p,LOG2E*r,(-0.5*LOG2E)*(u*p+v*r)+lo2,
            fs[6],fs[7],fs[8],fs[6],fs[7],fs[8],fs[6],fs[7],fs[8]]
        for k in range(15): xs[:,k,:]=cf[k]
        xs[:,15,:]=jnp.zeros_like(u)
        for c in range(3):
            ct=cot_ref[c:c+1,pl.ds(pl.multiple_of(ti*PIX,PIX),PIX)]
            h,m,l=split3(ct)
            for part in range(3):
                b=16*part+6+c
                rhs[b:b+1,PIX:]=h; rhs[b+3:b+4,PIX:]=m; rhs[b+6:b+7,PIX:]=l
        for c in range(3):
            cots[8*c:8*c+8,:]=jnp.broadcast_to(cot_ref[c:c+1,pl.ds(pl.multiple_of(ti*PIX,PIX),PIX)],(8,PIX))
        def slotp(tg,row0):
            for i in range(BU):
                x=xs[BU*tg+i]
                h,m,l=split3(x)
                y=jnp.concatenate([h,m,l,x,jnp.zeros((64,128),f32)],axis=0).T
                for k in range(8):
                    lhs[pl.ds(jnp.where(BU*tg+i<cnt,row0,4096),16,stride=8),:]=y[16*k:16*k+16,:]
                    row0=step_row(row0)
            return row0
        lax.fori_loop(0,(cnt+BU-1)//BU,slotp,0)
        rbs[...]=rhs[...].astype(bf16)
        def mm(b,h,dst):
            L=lhs[pl.ds(pl.multiple_of(b*128,128),128),0:48].astype(bf16)
            dst[...]=jnp.dot(L,rbs[:,h*PIX:h*PIX+PIX],preferred_element_type=f32)
        def fblock(b,src_):
            for jg in range(0,16,FJ):
                rows=[pl.ds(pl.multiple_of(b*128+8*jj,8),8) for jj in range(jg,jg+FJ)]
                cols=[]
                for rs in rows:
                    lrow=lhs[rs,:]
                    cols.append([jnp.broadcast_to(lrow[:,54+c:55+c],(8,128)) for c in range(3)])
                for i in range(7,-1,-1):
                    cs=slice(128*i,128*i+128)
                    T=st[0:8,cs]; I=[st[8+8*c:16+8*c,cs] for c in range(3)]
                    for m,rs in enumerate(rows):
                        aa=jnp.exp2(src_[8*(jg+m):8*(jg+m)+8,cs])
                        w=T*aa; T=T-w
                        for c in range(3): I[c]=I[c]+w*cols[m][c]
                        al[rs,cs]=aa; ws[rs,cs]=w
                    st[0:8,cs]=T
                    for c in range(3): st[8+8*c:16+8*c,cs]=I[c]
        st[0:8,:]=jnp.ones((8,PIX),f32)
        st[8:32,:]=jnp.zeros((24,PIX),f32)
        mm(0,0,eA)
        def fwd(b,_):
            nb=jnp.minimum(b+1,cnt-1)
            @pl.when(b%2==0)
            def _():
                mm(nb,0,eB); fblock(b,eA)
            @pl.when(b%2==1)
            def _():
                mm(nb,0,eA); fblock(b,eB)
            return 0
        lax.fori_loop(0,cnt,fwd,0)
        K=st[0:8,:]
        Cc=sum(st[8+8*c:16+8*c,:]*cots[8*c:8*c+8,:] for c in range(3))
        P=[jnp.ones((1,PIX),f32)]
        for s in range(7): P.append(P[-1]*K[s:s+1])
        V=[jnp.zeros((1,PIX),f32)]
        for s in range(7,0,-1): V.append(Cc[s:s+1]+K[s:s+1]*V[-1])
        Pv=jnp.concatenate(P,axis=0); V0=jnp.concatenate(V[::-1],axis=0)
        pref[...]=Pv
        lane128=lax.broadcasted_iota(jnp.int32,(8,128),1)//8
        def sums(sb_,zb_,r0):
            ra=jnp.dot(sb_[0:256],wa[...],preferred_element_type=f32)
            rc=jnp.dot(sb_[256:384],wb[...],preferred_element_type=f32)
            res[pl.ds(pl.multiple_of(r0,8),128),:]=ra[0:128]+ra[128:]+rc+zb_[...]
        def block(r0,qb,sb_,zb_):
            for jg in range(16-BJ,-1,-BJ):
                S=[[None]*3 for _ in range(BJ)]; Z=[[None]*3 for _ in range(BJ)]
                for i in range(7,-1,-1):
                    cs=slice(128*i,128*i+128)
                    V=vref[:,cs]; Pm=pref[:,cs]; ct=[cots[8*c:8*c+8,cs] for c in range(3)]
                    for m in range(BJ-1,-1,-1):
                        rs=pl.ds(pl.multiple_of(r0+8*(jg+m),8),8)
                        d=qb[8*(jg+m):8*(jg+m)+8,cs]-V
                        w=ws[rs,cs]*Pm
                        e=w*d
                        V=V+al[rs,cs]*d
                        for c in range(3):
                            zc=w*ct[c]
                            Z[m][c]=zc if i==7 else Z[m][c]+zc
                        s=S[m]
                        if i==7: s[0]=e; s[1]=e; s[2]=e
                        else:
                            s[0]=s[0]+e
                            if i>=1: s[1]=s[1]+s[0]; s[2]=s[2]+s[1]
                    vref[:,cs]=V
                for m in range(BJ):
                    zz=jnp.zeros((8,128),f32)
                    for c in range(3):
                        zz=jnp.where(lane128==6+c,jnp.sum(Z[m][c],axis=1,keepdims=True),zz)
                    zb_[8*(jg+m):8*(jg+m)+8,:]=zz
                for jp in range(0,BJ,2):
                    j=8*(jg+jp)
                    for m in range(3):
                        x=jnp.concatenate([S[jp][m],S[jp+1][m]],axis=0)
                        xh=x.astype(bf16); xl=(x-xh.astype(f32)).astype(bf16)
                        if m<2:
                            sb_[j:j+16,128*m:128*m+128]=xh
                            sb_[128+j:128+j+16,128*m:128*m+128]=xl
                        else:
                            sb_[256+j:256+j+16,0:128]=xh
                            sb_[256+j:256+j+16,128:256]=xl
        vref[...]=V0
        mm(cnt-1,1,eA)
        def bwd(i,_):
            b=cnt-1-i
            r0=pl.multiple_of(b*128,128)
            nb=jnp.maximum(b-1,0)
            @pl.when(i%2==0)
            def _():
                mm(nb,1,eB)
                sums(sbB,zbB,r0+128)
                block(r0,eA,sbA,zbA)
            @pl.when(i%2==1)
            def _():
                mm(nb,1,eA)
                sums(sbA,zbA,r0+128)
                block(r0,eB,sbB,zbB)
            return 0
        lax.fori_loop(0,cnt,bwd,0)
        @pl.when(cnt%2==1)
        def _(): sums(sbA,zbA,0)
        @pl.when(cnt%2==0)
        def _(): sums(sbB,zbB,0)
        sub=lax.broadcasted_iota(jnp.int32,(16,128),1)%8
        def slote(tg,row0):
            M=[None]*8
            for t in range(8):
                for k in range(8):
                    x=res[pl.ds(jnp.minimum(row0,last-1),16,stride=8),:]
                    M[k]=x if t==0 else jnp.where(sub==t,x,M[k])
                    row0=step_row(row0)
            Mt=jnp.concatenate(M,axis=0).T
            row=lambda k: Mt[8*k:8*k+8,:]
            mxx,mxy,myy,mx,my,m1=[row(k) for k in range(6)]
            tr=pl.ds(pl.multiple_of(8*tg,8),8)
            u=fs[0,tr,:]-cx; v=fs[1,tr,:]-cy; A=fs[2,tr,:]; B=fs[3,tr,:]; C=fs[4,tr,:]
            sx=mx-u*m1; sy=my-v*m1
            sxx=mxx-2.0*u*mx+u*u*m1
            syy=myy-2.0*v*my+v*v*m1
            sxy=mxy-u*my-v*mx+u*v*m1
            o=[A*sx+B*sy,B*sx+C*sy,-0.5*sxx,-sxy,-0.5*syy,m1]+[row(6+c) for c in range(3)]
            live=lax.broadcasted_iota(jnp.int32,(8,128),0)<cnt-8*tg
            o=[jnp.where(live,x,0.0) for x in o]
            for t in range(8):
                ow=jnp.right_shift(ints_ref[2*who,0,ti*32+8*tg+t],4)
                for f in range(9): out_ref[ow,f]=o[f][t:t+1,:]
            return row0
        lax.fori_loop(0,(cnt+7)//8,slote,0)
        return 0
    lax.fori_loop(0,8,tile,0)
def tiles(ints,feat,cot):
    sm=pl.BlockSpec(memory_space=pltpu.SMEM); vm=pl.BlockSpec(memory_space=pltpu.VMEM)
    return pl.pallas_call(tiles_kernel,out_shape=jax.ShapeDtypeStruct((2,128,9,1,128),f32),
        in_specs=[sm,vm,vm],out_specs=vm,
        scratch_shapes=[pltpu.VMEM((9,32,128),f32),pltpu.VMEM((32,16,128),f32),pltpu.VMEM((4096+128,128),f32),
            pltpu.VMEM((48,2*PIX),f32),pltpu.VMEM((256,128),bf16),pltpu.VMEM((256,128),bf16),pltpu.VMEM((8,PIX),f32),pltpu.VMEM((8,PIX),f32),
            pltpu.VMEM((32,PIX),f32),pltpu.VMEM((24,PIX),f32),pltpu.VMEM((48,2*PIX),bf16)]
            +[pltpu.VMEM((4096,PIX),f32)]*2+[pltpu.VMEM((128,PIX),f32)]*2
            +[pltpu.VMEM((384,256),bf16),pltpu.VMEM((128,128),f32)]*2+[pltpu.VMEM((4096+128,128),f32)],
        compiler_params=pltpu.CompilerParams(vmem_limit_bytes=67043328))(ints,feat,cot)


def load_params(p_ref):
    return [p_ref[row : row + 1, :].reshape(16, BLOCK) for row in range(59)]


def screen_rows(rows):
    return screen(rows, 1024.0, 512.0, 256.0)


LAG = 16


def everyone(me, n, act):
    def step(k, _):
        act(lax.rem(me + k, n))
        return 0

    lax.fori_loop(1, n, step, 0)


def lagged(me, n, fill, ship):
    def first(k, _):
        fill(lax.rem(me + k, n))
        return 0

    def both(k, _):
        fill(lax.rem(me + k, n))
        ship(lax.rem(me + k - LAG, n))
        return 0

    def last(k, _):
        ship(lax.rem(me + k, n))
        return 0

    lax.fori_loop(0, LAG + 1, first, 0)
    lax.fori_loop(LAG + 1, n, both, 0)
    lax.fori_loop(n - LAG, n, last, 0)


def send(src, dst, ssem, rsem, peer):
    return pltpu.make_async_remote_copy(
        src_ref=src,
        dst_ref=dst,
        send_sem=ssem,
        recv_sem=rsem,
        device_id=(peer,),
        device_id_type=pl.DeviceIdType.MESH,
    )


def all_but_one(ref, sem):
    rest = ref.at[pl.ds(0, ref.shape[0] - 1)]
    return pltpu.make_async_copy(rest, rest, sem)


def greet(me, n):
    bar = pltpu.get_barrier_semaphore()
    everyone(
        me,
        n,
        lambda peer: pl.semaphore_signal(bar, inc=1, device_id=(peer,), device_id_type=pl.DeviceIdType.MESH),
    )
    return bar


def forward_kernel(
    blk_ref, cnt_ref, p_ref, cot_ref, pair_ref, feat_ref, cot2_ref, idx_ref, ints_ref, lists, fsc, outbox, idxs, sems
):
    n = lax.axis_size("dev")
    me = lax.axis_index("dev")
    partner = me + 1 - 2 * lax.rem(me, 2)
    bar = greet(me, n)
    lane = lax.broadcasted_iota(jnp.int32, (1, 128), 1)
    ints_ref[0] = jnp.concatenate([blk_ref[k : k + 1, :] for k in range(4)], axis=1)
    ints_ref[1] = sum(jnp.where(lane == k, cnt_ref[k], 0) for k in range(4))
    for f, value in enumerate(screen_rows(load_params(p_ref))):
        fsc[f] = jnp.maximum(value, -1000.0) if f == 5 else value
    own_list = pltpu.make_async_copy(ints_ref.at[0], lists.at[me], sems.at[0])
    own_ints = pltpu.make_async_copy(ints_ref, pair_ref.at[pl.ds(0, 2)], sems.at[1])
    own_cot = pltpu.make_async_copy(cot_ref, cot2_ref.at[0], sems.at[2])
    own_list.start()
    own_ints.start()
    own_cot.start()
    pl.semaphore_wait(bar, n - 1)
    everyone(me, n, lambda peer: send(ints_ref.at[0], lists.at[me], sems.at[3], sems.at[4], peer).start())
    pair_ints = send(ints_ref, pair_ref.at[pl.ds(2, 2)], sems.at[5], sems.at[6], partner)
    pair_cot = send(cot_ref, cot2_ref.at[1], sems.at[7], sems.at[8], partner)
    pair_ints.start()
    pair_cot.start()
    own_list.wait()
    all_but_one(lists, sems.at[4]).wait()
    flat = lists[...].reshape(128, 128)
    asked = jnp.sum(jnp.where(flat >> 4 == me, flat & 15, 0).astype(f32), axis=1, keepdims=True)
    idx_ref[...] = jnp.broadcast_to(asked, (128, 128)).T[0:1].astype(jnp.int32)
    to_scalar = pltpu.make_async_copy(idx_ref, idxs, sems.at[9])
    to_scalar.start()
    to_scalar.wait()

    def put(d):
        for f in range(9):
            outbox[d, f] = fsc[f, pl.ds(idxs[0, d] & 15, 1), :]

    lagged(me, n, put, lambda peer: send(outbox.at[peer], feat_ref.at[0, me], sems.at[11], sems.at[12], peer).start())
    own_feat = pltpu.make_async_copy(outbox.at[me], feat_ref.at[0, me], sems.at[10])
    own_feat.start()
    all_but_one(lists, sems.at[3]).wait()
    own_ints.wait()
    own_cot.wait()
    own_feat.wait()
    pair_ints.wait()
    pair_cot.wait()
    all_but_one(outbox, sems.at[12]).wait()
    pair_feat = send(feat_ref.at[0], feat_ref.at[1], sems.at[13], sems.at[14], partner)
    pair_feat.start()
    all_but_one(outbox, sems.at[11]).wait()
    pair_feat.wait()


def back_kernel(grad_ref, recv_ref, theirs, outbox, sems):
    n = lax.axis_size("dev")
    me = lax.axis_index("dev")
    partner = me + 1 - 2 * lax.rem(me, 2)
    bar = greet(me, n)
    pl.semaphore_wait(bar, n - 1)
    pair = send(grad_ref.at[1], theirs, sems.at[0], sems.at[1], partner)
    pair.start()
    pair.wait_recv()

    def add(d):
        for f in range(9):
            outbox[d, f] = grad_ref[0, d, f] + theirs[d, f]

    lagged(me, n, add, lambda peer: send(outbox.at[peer], recv_ref.at[me], sems.at[3], sems.at[4], peer).start())
    own = pltpu.make_async_copy(outbox.at[me], recv_ref.at[me], sems.at[2])
    own.start()
    pair.wait_send()
    own.wait()
    all_but_one(outbox, sems.at[3]).wait()
    all_but_one(recv_ref, sems.at[4]).wait()


def final_kernel(idx_ref, p_ref, recv_ref, out_ref):
    rows = lax.broadcasted_iota(jnp.int32, (16, BLOCK), 0)

    def add(d, acc):
        hit = rows == idx_ref[0, d]
        return tuple(
            acc[f] + jnp.where(hit, jnp.broadcast_to(recv_ref[d, f], (16, BLOCK)), 0.0) for f in range(9)
        )

    zeros = tuple(jnp.zeros((16, BLOCK), f32) for _ in range(9))
    grads = list(lax.fori_loop(0, 128, add, zeros, unroll=4))
    pullback = jax.vjp(screen_rows, load_params(p_ref))[1]
    grads[5] = grads[5] * (1.0 / LOG2E)
    for row, value in enumerate(pullback(grads)[0]):
        out_ref[row : row + 1, :] = value.reshape(1, 2048)


def body(params, blocks, counts, pixel_grad):
    sm = pl.BlockSpec(memory_space=pltpu.SMEM)
    vm = pl.BlockSpec(memory_space=pltpu.VMEM)
    block_sums = jax.ShapeDtypeStruct((128, 9, 1, 128), f32)
    pair, feat, cot, idx = pl.pallas_call(
        forward_kernel,
        out_shape=[
            jax.ShapeDtypeStruct((4, 1, 128), jnp.int32),
            jax.ShapeDtypeStruct((2, 128, 9, 1, 128), f32),
            jax.ShapeDtypeStruct((2, 3, 4096), f32),
            jax.ShapeDtypeStruct((1, 128), jnp.int32),
        ],
        in_specs=[vm, sm, vm, vm],
        out_specs=[vm, vm, vm, vm],
        scratch_shapes=[
            pltpu.VMEM((2, 1, 128), jnp.int32),
            pltpu.VMEM((128, 1, 128), jnp.int32),
            pltpu.VMEM((9, 16, 128), f32),
            pltpu.VMEM((128, 9, 1, 128), f32),
            pltpu.SMEM((1, 128), jnp.int32),
            pltpu.SemaphoreType.DMA((15,)),
        ],
        compiler_params=pltpu.CompilerParams(collective_id=0, has_side_effects=True),
    )(blocks, counts, params, pixel_grad)
    grads = tiles(pair, feat, cot)
    back = pl.pallas_call(
        back_kernel,
        out_shape=block_sums,
        in_specs=[vm],
        out_specs=vm,
        scratch_shapes=[
            pltpu.VMEM((128, 9, 1, 128), f32),
            pltpu.VMEM((128, 9, 1, 128), f32),
            pltpu.SemaphoreType.DMA((5,)),
        ],
        compiler_params=pltpu.CompilerParams(collective_id=1, has_side_effects=True),
    )(grads)
    return pl.pallas_call(
        final_kernel,
        out_shape=jax.ShapeDtypeStruct((59, 2048), f32),
        in_specs=[sm, vm, vm],
        out_specs=vm,
    )(idx, params, back)


def solution(mesh):
    return jax.shard_map(
        body,
        mesh=mesh,
        in_specs=(P(None, "dev"), P("dev", None), P("dev"), P(None, "dev")),
        out_specs=P(None, "dev"),
        check_vma=False,
    )
```
